128 devices in a mesh: tg: 2 (over core), pw: 64 (over y, x, z).
Axes of the slice: x: 4, y: 4, z: 4, core: 2. Of those that a mesh axis runs over, the one named last changes fastest.
Arguments:
- coeffs: float32 [2, 32768, 256], P(None, ('tg', 'pw')), may hold values from -6 to 6
- g_place: int32 [32768], P(('tg', 'pw')), may hold values from 0 to 2047, as said below
- stick_column: int32 [2048], P(('tg', 'pw')), may hold values from 0 to 16383, as said below
- potential: float32 [128, 128, 128], P(None, None, ('tg', 'pw')), may hold values from -1 to 3
Outputs:
- hpsi: float32 [2, 32768, 256], P(None, ('tg', 'pw'))
The draws below stay inside these ranges and needn't reach their ends.
Inputs may be any that keep to these rules, and one draw needn't show every extreme that they name: g_place[g] = s * 128 + z: s is a stick slot of the owner g // 256, z a frequency within 32 of zero taken modulo 128; no two plane waves of one owner share s and z; each owner uses its slots 0 up to some count between 4 and 16, every one of them, and some owner uses all 16. `stick_column`: all stick slots name different columns x * 128 + y; with x and y read as signed frequencies (taken modulo 128), x * x + y * y <= 32 ** 2.
All inputs are finite; a program needn't handle non-finite values.
Results may differ from the reference program's by a relative error of at most 0.009.
Values may be sent and summed in bfloat16 or wider, within the bound.
No kernel may reach another device: no remote copies, remote signals or barrier semaphores. Data moves between devices by JAX's collectives and lax.ppermute only.
A program may use at most 128 MiB of HBM per device.

```python
import jax
import jax.numpy as jnp
from jax import lax

NR = 128
ZSPAN = 64
SLOT = 16
G_DEV = 256
BANDS = 256
G_TOTAL = 32768
STICKS = 2048


def live_slots(key):
    owners = STICKS // SLOT
    random_part = SLOT // 4 + jax.random.randint(jax.random.fold_in(key, 11), (owners,), 0, SLOT - SLOT // 4 + 1)
    busiest = jax.random.randint(jax.random.fold_in(key, 12), (), 0, owners)
    return jnp.where(jnp.arange(owners) == busiest, SLOT, random_part)


def draw_g_place(key, part):
    owners = STICKS // SLOT
    cell_count = SLOT * ZSPAN
    live_count = live_slots(key)
    position = jnp.arange(cell_count, dtype=jnp.int32)
    slot_of = position // ZSPAN
    random_part = jax.random.randint(jax.random.fold_in(key, 13), (owners, cell_count), 0, 2 ** 20)
    scores = random_part * cell_count + position[None, :]
    scores = jnp.where(position[None, :] % ZSPAN == 0, 2 ** 30 + position[None, :], scores)
    scores = jnp.where(slot_of[None, :] < live_count[:, None], scores, -1 - position[None, :])
    chosen = lax.top_k(scores, G_DEV)[1]
    frequency = chosen % ZSPAN - ZSPAN // 2
    placed = chosen // ZSPAN * NR + jnp.mod(frequency, NR)
    return placed.reshape(G_TOTAL).astype(jnp.int32)


def draw_stick_column(key, part):
    radius = ZSPAN // 2
    side_length = ZSPAN + 1
    cell_count = side_length * side_length
    position = jnp.arange(cell_count, dtype=jnp.int32)
    x_signed = position // side_length - radius
    y_signed = position % side_length - radius
    inside = x_signed * x_signed + y_signed * y_signed <= radius * radius
    random_part = jax.random.randint(jax.random.fold_in(key, 21), (cell_count,), 0, 2 ** 16)
    scores = jnp.where(inside, random_part * cell_count + position, -1 - position)
    chosen = lax.top_k(scores, STICKS)[1]
    x_index = jnp.mod(x_signed[chosen], NR)
    y_index = jnp.mod(y_signed[chosen], NR)
    return (x_index * NR + y_index).astype(jnp.int32)


def shard_levels(stream_key, extent, shards, low, high):
    def one(axis_at, parts):
        heights = jax.random.uniform(jax.random.fold_in(jax.random.fold_in(stream_key, 6), axis_at), (parts,), jnp.float32, low / len(shards), high / len(shards))
        return jnp.repeat(jnp.exp(heights), extent[axis_at] // parts).reshape((-1,) + (1,) * (len(extent) - axis_at - 1))

    level = one(*shards[0])
    for cut in shards[1:]:
        level = level * one(*cut)
    return level


def bell_draw(stream_key, shape, deviation, most, shards=(), kind=jnp.bfloat16):
    result = deviation * jax.random.normal(stream_key, shape, jnp.float32)
    if shards:
        result = result * shard_levels(stream_key, shape, shards, -0.22, 0.18)
    return jnp.clip(result, -most, most).astype(kind)


def setup_inputs(seed: int = 0) -> dict:
    seeds = jax.random.split(jax.random.key(seed), 5)
    return {
        "coeffs": bell_draw(seeds[0], (2, G_TOTAL, BANDS), 1.0, 6.0, ((1, 128),), jnp.float32),
        "g_place": draw_g_place(jax.random.fold_in(seeds[4], 71), 0),
        "stick_column": draw_stick_column(jax.random.fold_in(seeds[4], 71), 0),
        "potential": jnp.clip(-1.0 + 4.0 * jax.random.uniform(seeds[3], (NR, NR, NR), jnp.float32) ** shard_levels(seeds[3], (NR, NR, NR), ((2, 128),), -0.2, 0.2), -1.0, 3.0),
    }


def phase_table(left_index, right_index, sign_value, modulus):
    product = (left_index[:, None] * right_index[None, :]) % modulus
    angles = (2.0 * jnp.pi / modulus) * product.astype(jnp.float32)
    cosine = jnp.cos(angles)
    sine_part = sign_value * jnp.sin(angles)
    upper_row = jnp.stack([cosine, sine_part])
    lower_row = jnp.stack([-sine_part, cosine])
    return jnp.stack([upper_row, lower_row])


def plane_pass(lattice, volume, forward, inverse):
    ahead = forward.astype(jnp.float32)
    behind = inverse.astype(jnp.float32)
    partial_value = jnp.einsum('cxypb,cdyk->dxkpb', lattice.astype(jnp.float32), ahead).astype(jnp.bfloat16)
    psi_field = jnp.einsum('cxypb,cdxk->dkypb', partial_value.astype(jnp.float32), ahead)
    weighted = (psi_field * volume[None, :, :, :, None]).astype(jnp.bfloat16)
    reverse_half = jnp.einsum('cxypb,cdyk->dxkpb', weighted.astype(jnp.float32), behind).astype(jnp.bfloat16)
    return jnp.einsum('cxypb,cdxk->dkypb', reverse_half.astype(jnp.float32), behind)


def reference(coeffs, g_place, stick_column, potential):
    frequency = jnp.arange(NR, dtype=jnp.int32)
    forward = phase_table(frequency, frequency, 1.0, NR).astype(jnp.bfloat16)
    inverse = phase_table(frequency, frequency, -1.0, NR).astype(jnp.bfloat16)
    ahead_table = phase_table(frequency, frequency, 1.0, NR)
    return_table = phase_table(frequency, frequency, -1.0, NR)
    holder = (jnp.arange(G_TOTAL, dtype=jnp.int32) // G_DEV).astype(jnp.int32)
    flat_index = (holder * (SLOT * NR) + g_place).astype(jnp.int32)
    factor = 1.0 / NR ** 3

    def one_band(band_values):
        placed = jnp.zeros((2, STICKS * NR), jnp.float32).at[:, flat_index].add(band_values)
        placed = placed.reshape(2, STICKS, NR)
        sticks = jnp.einsum('csz,cdzk->dsk', placed, ahead_table, precision=lax.Precision.HIGHEST).astype(jnp.bfloat16)
        lattice = jnp.zeros((2, NR * NR, NR), jnp.bfloat16).at[:, stick_column].set(sticks)
        real_image = plane_pass(lattice.reshape(2, NR, NR, NR, 1), potential, forward, inverse)
        picked = real_image.reshape(2, NR * NR, NR)[:, stick_column].astype(jnp.bfloat16)
        spectra = jnp.einsum('csz,cdzk->dsk', picked.astype(jnp.float32), return_table, precision=lax.Precision.HIGHEST)
        return spectra.reshape(2, STICKS * NR)[:, flat_index] * factor

    stacked = lax.map(one_band, jnp.transpose(coeffs, (2, 0, 1)))
    return jnp.transpose(stacked, (1, 2, 0))
```

```python
import numpy as np
import jax
import jax.numpy as jnp
from jax import lax
from jax.experimental import pallas as pl
from jax.experimental.pallas import tpu as pltpu
from jax.sharding import Mesh
from jax.sharding import PartitionSpec as P

NR = 128
HALF = 32
BOX = 72
PAIRS = 33
SLOT = 16
LANES = 128
TG_PW = ("tg", "pw_0", "pw_1", "pw_2")
BF = jnp.bfloat16
F32 = jnp.float32
VMEM = pl.BlockSpec(memory_space=pltpu.VMEM)
SMEM = pl.BlockSpec(memory_space=pltpu.SMEM)


def complex_table(rows, cols, sign, keep_rows, keep_cols):
    angle = 2.0 * np.pi / NR * (np.outer(rows, cols) % NR)
    keep = keep_rows[:, None] * keep_cols[None, :]
    c = np.cos(angle) * keep
    s = sign * np.sin(angle) * keep
    return np.stack([np.stack([c, -s], 1), np.stack([s, c], 1)]).astype(np.float32)


def tables():
    full = np.arange(NR)
    box = np.arange(BOX) - HALF
    keep_box = (np.arange(BOX) <= 2 * HALF).astype(np.float32)
    keep_all = np.ones(NR, np.float32)
    ahead = complex_table(full, box, 1.0, keep_all, keep_box)
    behind = complex_table(box, full, -1.0, keep_box, keep_all)
    wide, tall = 2 * NR, 2 * BOX
    ahead_y = ahead.transpose(1, 0, 3, 2).reshape(wide, tall)
    ahead_x = ahead.reshape(wide, tall)
    behind_x = behind.reshape(tall, wide)
    behind_y = behind.transpose(1, 0, 3, 2).reshape(tall, wide)
    return [jnp.asarray(t, BF) for t in (ahead_y, ahead_x, behind_x, behind_y)]


def spread_kernel(c_ref, place_ref, info_ref, e_ref, a_ref, b_ref, t_ref):
    place = place_ref[...]
    row = (place >> 7) * BOX + ((place + HALF) & (NR - 1))
    at = lax.broadcasted_iota(jnp.int32, (SLOT * BOX, place.shape[1]), 0)
    select = jnp.where(at == row, 1.0, 0.0).astype(BF)
    parts = [
        jnp.dot(select, c_ref[p].astype(BF), preferred_element_type=F32) for p in range(2)
    ]
    for s in range(SLOT):
        x = jnp.concatenate([parts[p][s * BOX : (s + 1) * BOX] for p in range(2)], axis=0)
        m = jnp.dot(e_ref[...], x.astype(BF), preferred_element_type=F32)
        for h in range(2):
            for p in range(2):
                t_ref[h, pl.ds(2 * s + p, NR, stride=2 * SLOT), :] = m[
                    p * NR : (p + 1) * NR, h * LANES : (h + 1) * LANES
                ]
    info = jnp.broadcast_to(info_ref[...], (8, LANES)).astype(F32).astype(BF)

    @pl.loop(0, NR // 4)
    def _(i):
        for u in range(4):
            k = i * 4 + u
            rows = pl.ds(pl.multiple_of(k * 2 * SLOT, 2 * SLOT), 2 * SLOT)
            a_ref[k, 0 : 2 * SLOT, :] = t_ref[0, rows, :].astype(BF)
            a_ref[k, 2 * SLOT : 2 * SLOT + 8, :] = info
            b_ref[k] = t_ref[1, rows, :].astype(BF)


def spread(coeffs, place, info, ahead_z):
    return pl.pallas_call(
        spread_kernel,
        out_shape=(
            jax.ShapeDtypeStruct((NR, 2 * SLOT + 8, LANES), BF),
            jax.ShapeDtypeStruct((NR, 2 * SLOT, LANES), BF),
        ),
        in_specs=[VMEM] * 4,
        out_specs=(VMEM, VMEM),
        scratch_shapes=[pltpu.VMEM((2, NR * 2 * SLOT, LANES), F32)],
        compiler_params=pltpu.CompilerParams(vmem_limit_bytes=40 << 20),
        cost_estimate=pl.CostEstimate(
            flops=2 * (1152 * 256 * 512 + 4096 * 256 * 256), bytes_accessed=3 << 20, transcendentals=0
        ),
        name="spread",
    )(coeffs, place, info, ahead_z)


def plane_kernel(
    cell_ref, r_ref, v_ref, ey_ref, ex_ref, ix_ref, iy_ref, o_ref, f_ref, g_ref, s_ref, w_ref
):
    sticks = f_ref.shape[0] // 2
    owners = r_ref.shape[0]
    per = 2 * SLOT
    two = 2 * BOX
    blank = jnp.zeros((two, LANES), F32)

    @pl.loop(0, 2 * PAIRS)
    def _(x):
        g_ref[pl.ds(pl.multiple_of(x * two, 8), two), :] = blank

    @pl.loop(0, NR // 8)
    def _(i):
        for u in range(16):
            s_ref[pl.ds(pl.multiple_of((i * 16 + u) * BOX + 64, 8), 8), :] = blank[:8]

    @pl.loop(0, owners // 8)
    def _(i):
        for u in range(8):
            o = i * 8 + u
            f_ref[pl.ds(pl.multiple_of(o * per, per), per), :] = r_ref[o, 0:per, :].astype(F32)

    step = 32

    @pl.loop(0, sticks // step)
    def _(i):
        for u in range(step):
            c = cell_ref[i * step + u]
            g_ref[pl.ds(2 * c, 2), :] = f_ref[
                pl.ds(pl.multiple_of(i * 2 * step, 2 * step) + 2 * u, 2), :
            ]

    turn = 11

    @pl.loop(0, PAIRS // turn)
    def _(i):
        xs = []
        for u in range(turn):
            r0 = (i * turn + u) * 2 * two
            a = g_ref[pl.ds(pl.multiple_of(r0, 8), two), :].astype(BF)
            b = g_ref[pl.ds(pl.multiple_of(r0 + two, 8), two), :].astype(BF)
            xs.append(jnp.concatenate([a, b], axis=1))
        for u in range(turn):
            m = jnp.dot(ey_ref[...], xs[u], preferred_element_type=F32)
            x0 = 2 * (i * turn + u)
            s_ref[pl.ds(x0, 2 * NR, stride=BOX), :] = m[:, :LANES]
            s_ref[pl.ds(x0 + 1, 2 * NR, stride=BOX), :] = m[:, LANES:]

    lane = lax.broadcasted_iota(jnp.int32, (NR, NR), 1)
    v = v_ref[...]
    batch = 16

    @pl.loop(0, NR // 2 // batch)
    def _(i):
        xs = []
        for u in range(batch):
            r0 = (i * batch + u) * 2 * two
            a = s_ref[pl.ds(pl.multiple_of(r0, 8), two), :].astype(BF)
            b = s_ref[pl.ds(pl.multiple_of(r0 + two, 8), two), :].astype(BF)
            xs.append(jnp.concatenate([a, b], axis=1))
        for u in range(batch):
            psi = jnp.dot(ex_ref[...], xs[u], preferred_element_type=F32)
            q = 2 * (i * batch + u)
            vs = []
            for t in range(2):
                column = jnp.sum(jnp.where(lane == q + t, v, 0.0), axis=1, keepdims=True)
                vs.append(jnp.broadcast_to(column, (NR, LANES)))
            vv = jnp.concatenate(vs, axis=1)
            w_ref[u] = (psi * jnp.concatenate([vv, vv], axis=0)).astype(BF)
        for u in range(batch):
            h = jnp.dot(ix_ref[...], w_ref[u], preferred_element_type=F32)
            r0 = (i * batch + u) * 2 * two
            s_ref[pl.ds(pl.multiple_of(r0, 8), two), :] = h[:, :LANES]
            s_ref[pl.ds(pl.multiple_of(r0 + two, 8), two), :] = h[:, LANES:]

    @pl.loop(0, PAIRS // turn)
    def _(i):
        xs = []
        for u in range(turn):
            x0 = 2 * (i * turn + u)
            a = s_ref[pl.ds(x0, 2 * NR, stride=BOX), :].astype(BF)
            b = s_ref[pl.ds(x0 + 1, 2 * NR, stride=BOX), :].astype(BF)
            xs.append(jnp.concatenate([a, b], axis=1))
        for u in range(turn):
            m = jnp.dot(iy_ref[...], xs[u], preferred_element_type=F32)
            r0 = (i * turn + u) * 2 * two
            g_ref[pl.ds(pl.multiple_of(r0, 8), two), :] = m[:, :LANES]
            g_ref[pl.ds(pl.multiple_of(r0 + two, 8), two), :] = m[:, LANES:]

    @pl.loop(0, sticks // step)
    def _(i):
        for u in range(step):
            c = cell_ref[i * step + u]
            f_ref[pl.ds(pl.multiple_of(i * 2 * step, 2 * step) + 2 * u, 2), :] = g_ref[
                pl.ds(2 * c, 2), :
            ]

    @pl.loop(0, owners // 8)
    def _(i):
        for u in range(8):
            o = i * 8 + u
            o_ref[o] = f_ref[pl.ds(pl.multiple_of(o * per, per), per), :].astype(BF)


def plane_pass(cells, received, volume, tabs):
    owners = received.shape[0]
    return pl.pallas_call(
        plane_kernel,
        out_shape=jax.ShapeDtypeStruct((owners, 2 * SLOT, LANES), BF),
        in_specs=[SMEM] + [VMEM] * 6,
        out_specs=VMEM,
        scratch_shapes=[
            pltpu.VMEM((owners * 2 * SLOT, LANES), F32),
            pltpu.VMEM((2 * PAIRS * 2 * BOX, LANES), F32),
            pltpu.VMEM((2 * NR * BOX, LANES), F32),
            pltpu.VMEM((16, 2 * NR, 2 * LANES), BF),
        ],
        compiler_params=pltpu.CompilerParams(vmem_limit_bytes=40 << 20),
        cost_estimate=pl.CostEstimate(
            flops=2 * 38500 * 256 * 256, bytes_accessed=3 << 20, transcendentals=0
        ),
        name="plane",
    )(cells, received, volume, *tabs)


def finish_kernel(r_ref, place_ref, i_ref, *rest):
    o_ref, t_ref, sp_ref = rest[-3:]
    per = 2 * SLOT

    @pl.loop(0, NR // 8)
    def _(i):
        for u in range(8):
            k = i * 8 + u
            t_ref[pl.ds(pl.multiple_of(k * per, per), per), :] = r_ref[k].astype(F32)

    for j in range(SLOT // 2):
        pair = [
            jnp.concatenate(
                [t_ref[pl.ds(2 * (2 * j + q) + p, NR, stride=per), :] for p in range(2)], axis=0
            )
            for q in range(2)
        ]
        x = jnp.concatenate(pair, axis=1).astype(BF)
        m = jnp.dot(i_ref[...], x, preferred_element_type=F32)
        for q in range(2):
            rows = pl.ds((2 * j + q) * BOX, BOX)
            for p in range(2):
                sp_ref[rows, p * LANES : (p + 1) * LANES] = m[
                    p * BOX : (p + 1) * BOX, q * LANES : (q + 1) * LANES
                ]
    place = place_ref[...]
    row = (place >> 7) * BOX + ((place + HALF) & (NR - 1))
    at = lax.broadcasted_iota(jnp.int32, (place.shape[0], SLOT * BOX), 1)
    select = jnp.where(at == row, 1.0 / NR**3, 0.0).astype(BF)
    out = jnp.dot(select, sp_ref[...].astype(BF), preferred_element_type=F32)
    for p in range(2):
        o_ref[p] = out[:, p * LANES : (p + 1) * LANES]


def finish(returned, place, behind_z, half, into=None):
    count = place.shape[0]
    extra = [] if into is None else [into]
    return pl.pallas_call(
        finish_kernel,
        grid=(1,),
        out_shape=jax.ShapeDtypeStruct((2, count, 2 * LANES), F32),
        in_specs=[VMEM] * 3 + [pl.BlockSpec(memory_space=pl.ANY)] * len(extra),
        out_specs=pl.BlockSpec((2, count, LANES), lambda i: (0, 0, half)),
        scratch_shapes=[
            pltpu.VMEM((NR * 2 * SLOT, LANES), F32),
            pltpu.VMEM((SLOT * BOX, 2 * LANES), F32),
        ],
        input_output_aliases={} if into is None else {3: 0},
        compiler_params=pltpu.CompilerParams(vmem_limit_bytes=24 << 20),
        cost_estimate=pl.CostEstimate(
            flops=2 * (1152 + 1280) * 256 * 256, bytes_accessed=2 << 20, transcendentals=0
        ),
        name="finish",
    )(returned, place, behind_z, *extra)


def exchange(value):
    return lax.all_to_all(value, TG_PW, split_axis=0, concat_axis=0, tiled=True)


def body(coeffs, g_place, stick_column, potential):
    tabs = tables()
    ahead_z, behind_z = tabs[1], tabs[2]
    x_box = ((stick_column >> 7) + HALF) & (NR - 1)
    y_box = (stick_column + HALF) & (NR - 1)
    info = jnp.pad(jnp.concatenate([x_box, y_box]), (0, LANES - 2 * SLOT)).reshape(1, LANES)
    sent_a, sent_b = spread(coeffs, g_place.reshape(1, -1), info, ahead_z)
    got_a = exchange(sent_a)
    got_b = exchange(sent_b)
    column = got_a[:, 2 * SLOT, : 2 * SLOT].astype(F32).astype(jnp.int32)
    cells = (column[:, :SLOT] * BOX + column[:, SLOT:]).reshape(-1)
    volume = potential.reshape(NR, NR)
    done_a = plane_pass(cells, got_a, volume, tabs)
    back_a = exchange(done_a)
    done_b = plane_pass(cells, got_b, volume, tabs)
    back_b = exchange(done_b)
    place = g_place.reshape(-1, 1)
    out = finish(back_a, place, behind_z, 0)
    return finish(back_b, place, behind_z, 1, out)


def solution(mesh):
    torus = Mesh(mesh.devices.reshape(mesh.shape["tg"], 4, 4, 4), ("tg", "pw_0", "pw_1", "pw_2"))
    return jax.shard_map(
        body,
        mesh=torus,
        in_specs=(P(None, TG_PW, None), P(TG_PW), P(TG_PW), P(None, None, TG_PW)),
        out_specs=P(None, TG_PW, None),
        check_vma=False,
    )
```

```python
import functools

import numpy as np
import jax
import jax.numpy as jnp
from jax import lax
from jax.experimental import pallas as pl
from jax.experimental.pallas import tpu as pltpu
from jax.sharding import Mesh
from jax.sharding import PartitionSpec as P

NR = 128
HALF = 32
BOX = 72
PAIRS = 33
SLOT = 16
LANES = 128
PIECES = 4
TG_PW = ("tg", "pw_0", "pw_1", "pw_2")
BF = jnp.bfloat16
F32 = jnp.float32
VMEM = pl.BlockSpec(memory_space=pltpu.VMEM)
HBM = pl.BlockSpec(memory_space=pltpu.HBM)
SMEM = pl.BlockSpec(memory_space=pltpu.SMEM)


def complex_table(rows, cols, sign, keep_rows, keep_cols):
    angle = 2.0 * np.pi / NR * (np.outer(rows, cols) % NR)
    keep = keep_rows[:, None] * keep_cols[None, :]
    c = np.cos(angle) * keep
    s = sign * np.sin(angle) * keep
    return np.stack([np.stack([c, -s], 1), np.stack([s, c], 1)]).astype(np.float32)


def tables():
    full = np.arange(NR)
    box = np.arange(BOX) - HALF
    keep_box = (np.arange(BOX) <= 2 * HALF).astype(np.float32)
    keep_all = np.ones(NR, np.float32)
    ahead = complex_table(full, box, 1.0, keep_all, keep_box)
    behind = complex_table(box, full, -1.0, keep_box, keep_all)
    wide, tall = 2 * NR, 2 * BOX
    ahead_y = ahead.transpose(1, 0, 3, 2).reshape(wide, tall)
    ahead_x = ahead.reshape(wide, tall)
    behind_x = behind.reshape(tall, wide)
    behind_y = behind.transpose(1, 0, 3, 2).reshape(tall, wide)
    return [jnp.asarray(t, BF) for t in (ahead_y, ahead_x, behind_x, behind_y)]


def spread_kernel(
    half, c_hbm, place_hbm, column_ref, e_hbm, o_ref, c_ref, place_ref, e_ref, t_ref, sem
):
    first = pltpu.make_async_copy(place_hbm, place_ref, sem.at[2])
    first.start()
    copies = [
        pltpu.make_async_copy(
            c_hbm.at[p, :, pl.ds(half * LANES, LANES)], c_ref.at[p], sem.at[p]
        )
        for p in range(2)
    ]
    copies.append(pltpu.make_async_copy(e_hbm, e_ref, sem.at[3]))
    for copy in copies:
        copy.start()
    first.wait()
    place = place_ref[...]
    row = (place >> 7) * BOX + ((place + HALF) & (NR - 1))
    at = lax.broadcasted_iota(jnp.int32, (SLOT * BOX, place.shape[1]), 0)
    select = jnp.where(at == row, 1.0, 0.0).astype(BF)
    for copy in copies:
        copy.wait()
    both = jnp.concatenate([c_ref[p].astype(BF) for p in range(2)], axis=1)
    placed = jnp.dot(select, both, preferred_element_type=F32)
    xs = []
    for s in range(SLOT):
        rows = placed[s * BOX : (s + 1) * BOX]
        xs.append(jnp.concatenate([rows[:, :LANES], rows[:, LANES:]], axis=0).astype(BF))
    for j in range(SLOT // 2):
        x = jnp.concatenate(xs[2 * j : 2 * j + 2], axis=1)
        m = jnp.dot(e_ref[...], x, preferred_element_type=F32)
        for q in range(2):
            for p in range(2):
                t_ref[pl.ds(2 * (2 * j + q) + p, NR, stride=2 * SLOT), :] = m[
                    p * NR : (p + 1) * NR, q * LANES : (q + 1) * LANES
                ]
    if half == 0:
        lane = lax.broadcasted_iota(jnp.int32, (8, LANES), 1)
        info = jnp.zeros((8, LANES), jnp.int32)
        for s in range(SLOT):
            column = column_ref[s]
            info = jnp.where(lane == s, ((column >> 7) + HALF) & (NR - 1), info)
            info = jnp.where(lane == SLOT + s, (column + HALF) & (NR - 1), info)
        info = info.astype(F32).astype(BF)

    @pl.loop(0, NR // 8)
    def _(i):
        for u in range(8):
            k = i * 8 + u
            rows = pl.ds(pl.multiple_of(k * 2 * SLOT, 2 * SLOT), 2 * SLOT)
            o_ref[k, 0 : 2 * SLOT, :] = t_ref[rows, :].astype(BF)
            if half == 0:
                o_ref[k, 2 * SLOT : 2 * SLOT + 8, :] = info


def spread(half, coeffs, place, columns, ahead_z):
    height = 2 * SLOT + (8 if half == 0 else 0)
    return pl.pallas_call(
        functools.partial(spread_kernel, half),
        out_shape=jax.ShapeDtypeStruct((NR, height, LANES), BF),
        in_specs=[HBM, HBM, SMEM, HBM],
        out_specs=VMEM,
        scratch_shapes=[
            pltpu.VMEM((2, place.shape[1], LANES), F32),
            pltpu.VMEM(place.shape, jnp.int32),
            pltpu.VMEM(ahead_z.shape, BF),
            pltpu.VMEM((NR * 2 * SLOT, LANES), F32),
            pltpu.SemaphoreType.DMA((4,)),
        ],
        compiler_params=pltpu.CompilerParams(vmem_limit_bytes=62 << 20),
        cost_estimate=pl.CostEstimate(
            flops=2 * (1152 + 2048) * 256 * 256, bytes_accessed=2 << 20, transcendentals=0
        ),
        name="spread",
    )(coeffs, place, columns, ahead_z)


def plane_kernel(
    cell_ref, r_hbm, v_hbm, ey_hbm, ex_hbm, ix_hbm, iy_hbm, o_hbm,
    r_ref, v_ref, ey_ref, ex_ref, ix_ref, iy_ref, f_ref, g_ref, s_ref, w_ref, sem,
):
    sticks = f_ref.shape[0] // 2
    owners = r_ref.shape[0]
    per = 2 * SLOT
    two = 2 * BOX
    share = owners // PIECES
    pieces = [
        pltpu.make_async_copy(
            r_hbm.at[pl.ds(q * share, share), pl.ds(0, per), :],
            r_ref.at[pl.ds(q * share, share)],
            sem.at[q],
        )
        for q in range(PIECES)
    ]
    fixed = [
        pltpu.make_async_copy(src, dst, sem.at[PIECES + n])
        for n, (src, dst) in enumerate(
            [(ey_hbm, ey_ref), (v_hbm, v_ref), (ex_hbm, ex_ref), (ix_hbm, ix_ref), (iy_hbm, iy_ref)]
        )
    ]
    for copy in pieces + fixed:
        copy.start()
    blank = jnp.zeros((two, LANES), F32)

    @pl.loop(0, PAIRS)
    def _(x):
        g_ref[pl.ds(pl.multiple_of(x * 2 * two, 8), two), :] = blank
        g_ref[pl.ds(pl.multiple_of(x * 2 * two + two, 8), two), :] = blank

    @pl.loop(0, NR // 16)
    def _(i):
        for u in range(32):
            s_ref[pl.ds(pl.multiple_of((i * 32 + u) * BOX + 64, 8), 8), :] = blank[:8]

    step = 32
    for q in range(PIECES):
        pieces[q].wait()

        @pl.loop(q * share // 8, (q + 1) * share // 8)
        def _(i):
            for u in range(8):
                o = i * 8 + u
                f_ref[pl.ds(pl.multiple_of(o * per, per), per), :] = r_ref[o].astype(F32)

        @pl.loop(q * sticks // PIECES // step, (q + 1) * sticks // PIECES // step)
        def _(i):
            for u in range(step):
                c = cell_ref[i * step + u]
                g_ref[pl.ds(2 * c, 2), :] = f_ref[
                    pl.ds(pl.multiple_of(i * 2 * step, 2 * step) + 2 * u, 2), :
                ]

    for copy in fixed:
        copy.wait()
    turn = 11

    @pl.loop(0, PAIRS // turn)
    def _(i):
        xs = []
        for u in range(turn):
            r0 = (i * turn + u) * 2 * two
            a = g_ref[pl.ds(pl.multiple_of(r0, 8), two), :].astype(BF)
            b = g_ref[pl.ds(pl.multiple_of(r0 + two, 8), two), :].astype(BF)
            xs.append(jnp.concatenate([a, b], axis=1))
        for u in range(turn):
            m = jnp.dot(ey_ref[...], xs[u], preferred_element_type=F32)
            x0 = 2 * (i * turn + u)
            s_ref[pl.ds(x0, 2 * NR, stride=BOX), :] = m[:, :LANES]
            s_ref[pl.ds(x0 + 1, 2 * NR, stride=BOX), :] = m[:, LANES:]

    lane = lax.broadcasted_iota(jnp.int32, (NR, NR), 1)
    v = v_ref[...]
    batch = 16

    @pl.loop(0, NR // 2 // batch)
    def _(i):
        xs = []
        for u in range(batch):
            r0 = (i * batch + u) * 2 * two
            a = s_ref[pl.ds(pl.multiple_of(r0, 8), two), :].astype(BF)
            b = s_ref[pl.ds(pl.multiple_of(r0 + two, 8), two), :].astype(BF)
            xs.append(jnp.concatenate([a, b], axis=1))
        for u in range(batch):
            psi = jnp.dot(ex_ref[...], xs[u], preferred_element_type=F32)
            q = 2 * (i * batch + u)
            vs = []
            for t in range(2):
                column = jnp.sum(jnp.where(lane == q + t, v, 0.0), axis=1, keepdims=True)
                vs.append(jnp.broadcast_to(column, (NR, LANES)))
            vv = jnp.concatenate(vs, axis=1)
            w_ref[u] = (psi * jnp.concatenate([vv, vv], axis=0)).astype(BF)
        for u in range(batch):
            h = jnp.dot(ix_ref[...], w_ref[u], preferred_element_type=F32)
            r0 = (i * batch + u) * 2 * two
            s_ref[pl.ds(pl.multiple_of(r0, 8), two), :] = h[:, :LANES]
            s_ref[pl.ds(pl.multiple_of(r0 + two, 8), two), :] = h[:, LANES:]

    @pl.loop(0, PAIRS // turn)
    def _(i):
        xs = []
        for u in range(turn):
            x0 = 2 * (i * turn + u)
            a = s_ref[pl.ds(x0, 2 * NR, stride=BOX), :].astype(BF)
            b = s_ref[pl.ds(x0 + 1, 2 * NR, stride=BOX), :].astype(BF)
            xs.append(jnp.concatenate([a, b], axis=1))
        for u in range(turn):
            m = jnp.dot(iy_ref[...], xs[u], preferred_element_type=F32)
            r0 = (i * turn + u) * 2 * two
            g_ref[pl.ds(pl.multiple_of(r0, 8), two), :] = m[:, :LANES]
            g_ref[pl.ds(pl.multiple_of(r0 + two, 8), two), :] = m[:, LANES:]

    backs = []
    for q in range(PIECES):

        @pl.loop(q * sticks // PIECES // step, (q + 1) * sticks // PIECES // step)
        def _(i):
            for u in range(step):
                c = cell_ref[i * step + u]
                f_ref[pl.ds(pl.multiple_of(i * 2 * step, 2 * step) + 2 * u, 2), :] = g_ref[
                    pl.ds(2 * c, 2), :
                ]

        @pl.loop(q * share // 8, (q + 1) * share // 8)
        def _(i):
            for u in range(8):
                o = i * 8 + u
                r_ref[o] = f_ref[pl.ds(pl.multiple_of(o * per, per), per), :].astype(BF)

        part = pl.ds(q * share, share)
        backs.append(pltpu.make_async_copy(r_ref.at[part], o_hbm.at[part], sem.at[q]))
        backs[q].start()
    for copy in backs:
        copy.wait()


def plane_pass(cells, received, volume, tabs):
    owners = received.shape[0]
    return pl.pallas_call(
        plane_kernel,
        out_shape=jax.ShapeDtypeStruct((owners, 2 * SLOT, LANES), BF),
        in_specs=[SMEM] + [HBM] * 6,
        out_specs=HBM,
        scratch_shapes=[
            pltpu.VMEM((owners, 2 * SLOT, LANES), BF),
            pltpu.VMEM(volume.shape, F32),
            *[pltpu.VMEM(t.shape, BF) for t in tabs],
            pltpu.VMEM((owners * 2 * SLOT, LANES), F32),
            pltpu.VMEM((2 * PAIRS * 2 * BOX, LANES), F32),
            pltpu.VMEM((2 * NR * BOX, LANES), F32),
            pltpu.VMEM((16, 2 * NR, 2 * LANES), BF),
            pltpu.SemaphoreType.DMA((PIECES + 5,)),
        ],
        compiler_params=pltpu.CompilerParams(vmem_limit_bytes=62 << 20),
        cost_estimate=pl.CostEstimate(
            flops=2 * 38500 * 256 * 256, bytes_accessed=3 << 20, transcendentals=0
        ),
        name="plane",
    )(cells, received, volume, *tabs)


def finish_kernel(half, r_ref, place_ref, i_ref, *rest):
    o_hbm, t_ref, sp_ref, out_ref, sem = rest[-5:]
    per = 2 * SLOT
    place = place_ref[...]
    row = (place >> 7) * BOX + ((place + HALF) & (NR - 1))
    at = lax.broadcasted_iota(jnp.int32, (place.shape[0], SLOT * BOX), 1)
    select = jnp.where(at == row, 1.0 / NR**3, 0.0).astype(BF)

    @pl.loop(0, NR // 8)
    def _(i):
        for u in range(8):
            k = i * 8 + u
            t_ref[pl.ds(pl.multiple_of(k * per, per), per), :] = r_ref[k].astype(F32)

    for j in range(SLOT // 2):
        pair = [
            jnp.concatenate(
                [t_ref[pl.ds(2 * (2 * j + q) + p, NR, stride=per), :] for p in range(2)], axis=0
            )
            for q in range(2)
        ]
        x = jnp.concatenate(pair, axis=1).astype(BF)
        m = jnp.dot(i_ref[...], x, preferred_element_type=F32)
        for q in range(2):
            rows = pl.ds((2 * j + q) * BOX, BOX)
            for p in range(2):
                sp_ref[rows, p * LANES : (p + 1) * LANES] = m[
                    p * BOX : (p + 1) * BOX, q * LANES : (q + 1) * LANES
                ]
    out = jnp.dot(select, sp_ref[...].astype(BF), preferred_element_type=F32)
    sends = []
    for p in range(2):
        out_ref[p] = out[:, p * LANES : (p + 1) * LANES]
        sends.append(
            pltpu.make_async_copy(
                out_ref.at[p], o_hbm.at[p, :, pl.ds(half * LANES, LANES)], sem.at[p]
            )
        )
        sends[p].start()
    for copy in sends:
        copy.wait()


def finish(returned, place, behind_z, half, into=None):
    count = place.shape[0]
    extra = [] if into is None else [into]
    return pl.pallas_call(
        functools.partial(finish_kernel, half),
        out_shape=jax.ShapeDtypeStruct((2, count, 2 * LANES), F32),
        in_specs=[VMEM] * 3 + [HBM] * len(extra),
        out_specs=HBM,
        scratch_shapes=[
            pltpu.VMEM((NR * 2 * SLOT, LANES), F32),
            pltpu.VMEM((SLOT * BOX, 2 * LANES), F32),
            pltpu.VMEM((2, count, LANES), F32),
            pltpu.SemaphoreType.DMA((2,)),
        ],
        input_output_aliases={} if into is None else {3: 0},
        compiler_params=pltpu.CompilerParams(vmem_limit_bytes=24 << 20),
        cost_estimate=pl.CostEstimate(
            flops=2 * (1152 + 1280) * 256 * 256, bytes_accessed=2 << 20, transcendentals=0
        ),
        name="finish",
    )(returned, place, behind_z, *extra)


def exchange(value):
    return lax.all_to_all(value, TG_PW, split_axis=0, concat_axis=0, tiled=True)


def body(coeffs, g_place, stick_column, potential):
    tabs = tables()
    ahead_z, behind_z = tabs[1], tabs[2]
    row = g_place.reshape(1, -1)
    sent_a = spread(0, coeffs, row, stick_column, ahead_z)
    sent_b = spread(1, coeffs, row, stick_column, ahead_z)
    got_a = exchange(sent_a)
    got_b = exchange(sent_b)
    volume = potential.reshape(NR, NR)
    column = got_a[:, 2 * SLOT, : 2 * SLOT].astype(F32).astype(jnp.int32)
    cells = (column[:, :SLOT] * BOX + column[:, SLOT:]).reshape(-1)
    done_a = plane_pass(cells, got_a, volume, tabs)
    back_a = exchange(done_a)
    done_b = plane_pass(cells, got_b, volume, tabs)
    back_b = exchange(done_b)
    place = g_place.reshape(-1, 1)
    out = finish(back_a, place, behind_z, 0)
    return finish(back_b, place, behind_z, 1, out)


def solution(mesh):
    torus = Mesh(mesh.devices.reshape(mesh.shape["tg"], 4, 4, 4), ("tg", "pw_0", "pw_1", "pw_2"))
    return jax.shard_map(
        body,
        mesh=torus,
        in_specs=(P(None, TG_PW, None), P(TG_PW), P(TG_PW), P(None, None, TG_PW)),
        out_specs=P(None, TG_PW, None),
        check_vma=False,
    )
```

```python
import functools

import numpy as np
import jax
import jax.numpy as jnp
from jax import lax
from jax.experimental import pallas as pl
from jax.experimental.pallas import tpu as pltpu
from jax.sharding import Mesh
from jax.sharding import PartitionSpec as P

NR = 128
HALF = 32
BOX = 72
SIDE = 65
SLOT = 16
LANES = 128
PER = 4 * SLOT
PIECES = 4
TG_PW = ("tg", "pw_0", "pw_1", "pw_2")
BF = jnp.bfloat16
F32 = jnp.float32
VMEM = pl.BlockSpec(memory_space=pltpu.VMEM)
HBM = pl.BlockSpec(memory_space=pltpu.HBM)
SMEM = pl.BlockSpec(memory_space=pltpu.SMEM)


def complex_table(rows, cols, sign, keep_rows, keep_cols):
    angle = 2.0 * np.pi / NR * (np.outer(rows, cols) % NR)
    keep = keep_rows[:, None] * keep_cols[None, :]
    c = np.cos(angle) * keep
    s = sign * np.sin(angle) * keep
    return np.stack([np.stack([c, -s], 1), np.stack([s, c], 1)]).astype(np.float32)


def tables():
    full = np.arange(NR)
    box = np.arange(BOX) - HALF
    keep_box = (np.arange(BOX) <= 2 * HALF).astype(np.float32)
    keep_all = np.ones(NR, np.float32)
    ahead = complex_table(full, box, 1.0, keep_all, keep_box)
    behind = complex_table(box, full, -1.0, keep_box, keep_all)
    wide, tall = 2 * NR, 2 * BOX
    ahead_x = ahead.reshape(wide, tall)
    behind_x = behind.reshape(tall, wide)
    behind_y = behind.transpose(0, 1, 3, 2).reshape(tall, wide)
    ahead_y = ahead.transpose(1, 0, 2, 3).reshape(wide, tall)
    return [jnp.asarray(t, BF) for t in (ahead_x, behind_x, behind_y, ahead_y)]


def spread_kernel(
    c_hbm, place_hbm, column_ref, e_hbm, o_hbm, c_ref, place_ref, e_ref, t_ref, o_ref, sem
):
    first = pltpu.make_async_copy(place_hbm, place_ref, sem.at[PIECES])
    first.start()
    copies = [pltpu.make_async_copy(c_hbm.at[p], c_ref.at[p], sem.at[p]) for p in range(2)]
    copies.append(pltpu.make_async_copy(e_hbm, e_ref, sem.at[2]))
    for copy in copies:
        copy.start()
    first.wait()
    place = place_ref[...]
    row = (place >> 7) * BOX + ((place + HALF) & (NR - 1))
    at = lax.broadcasted_iota(jnp.int32, (SLOT * BOX, place.shape[1]), 0)
    select = jnp.where(at == row, 1.0, 0.0).astype(BF)
    lane = lax.broadcasted_iota(jnp.int32, (8, LANES), 1)
    info = jnp.zeros((8, LANES), jnp.int32)
    for s in range(SLOT):
        column = column_ref[s]
        info = jnp.where(lane == s, ((column >> 7) + HALF) & (NR - 1), info)
        info = jnp.where(lane == SLOT + s, (column + HALF) & (NR - 1), info)
    info = info.astype(F32).astype(BF)
    for copy in copies:
        copy.wait()
    both = jnp.concatenate([c_ref[p].astype(BF) for p in range(2)], axis=1)
    placed = jnp.dot(select, both, preferred_element_type=F32)
    xs = []
    for s in range(SLOT):
        rows = placed[s * BOX : (s + 1) * BOX]
        xs.append(
            jnp.concatenate([rows[:, : 2 * LANES], rows[:, 2 * LANES :]], axis=0).astype(BF)
        )
    for s in range(SLOT):
        m = jnp.dot(e_ref[...], xs[s], preferred_element_type=F32)
        for h in range(2):
            for p in range(2):
                t_ref[pl.ds(4 * s + 2 * h + p, NR, stride=PER), :] = m[
                    p * NR : (p + 1) * NR, h * LANES : (h + 1) * LANES
                ]
    share = NR // PIECES
    sends = []
    for q in range(PIECES):

        @pl.loop(q * share // 4, (q + 1) * share // 4)
        def _(i):
            for u in range(4):
                k = i * 4 + u
                rows = pl.ds(pl.multiple_of(k * PER, PER), PER)
                o_ref[k, 0:PER, :] = t_ref[rows, :].astype(BF)
                o_ref[k, PER : PER + 8, :] = info

        part = pl.ds(q * share, share)
        sends.append(pltpu.make_async_copy(o_ref.at[part], o_hbm.at[part], sem.at[q]))
        sends[q].start()
    for copy in sends:
        copy.wait()


def spread(coeffs, place, columns, ahead_z):
    out = jax.ShapeDtypeStruct((NR, PER + 8, LANES), BF)
    return pl.pallas_call(
        spread_kernel,
        out_shape=out,
        in_specs=[HBM, HBM, SMEM, HBM],
        out_specs=HBM,
        scratch_shapes=[
            pltpu.VMEM(coeffs.shape, F32),
            pltpu.VMEM(place.shape, jnp.int32),
            pltpu.VMEM(ahead_z.shape, BF),
            pltpu.VMEM((NR * PER, LANES), F32),
            pltpu.VMEM(out.shape, BF),
            pltpu.SemaphoreType.DMA((PIECES + 1,)),
        ],
        compiler_params=pltpu.CompilerParams(vmem_limit_bytes=62 << 20),
        cost_estimate=pl.CostEstimate(
            flops=2 * (2304 + 4096) * 256 * 256, bytes_accessed=3 << 20, transcendentals=0
        ),
        name="spread",
    )(coeffs, place, columns, ahead_z)


def plane_kernel(
    cell_ref, r_in, v_hbm, ey_hbm, ex_hbm, ix_hbm, iy_hbm, o_ref,
    v_ref, ey_ref, ex_ref, ix_ref, iy_ref, f_ref, g_ref, s_ref, w_ref, sem,
):
    owners = o_ref.shape[0]
    sticks = owners * SLOT
    tall = 2 * BOX
    share = owners // PIECES
    fixed = [
        pltpu.make_async_copy(src, dst, sem.at[n])
        for n, (src, dst) in enumerate(
            [(ey_hbm, ey_ref), (v_hbm, v_ref), (ex_hbm, ex_ref), (ix_hbm, ix_ref), (iy_hbm, iy_ref)]
        )
    ]
    for copy in fixed:
        copy.start()
    blank = jnp.zeros((4 * BOX, LANES), F32)

    @pl.loop(0, SIDE)
    def _(x):
        g_ref[pl.ds(pl.multiple_of(x * 4 * BOX, 8), 4 * BOX), :] = blank

    @pl.loop(0, NR // 8)
    def _(i):
        for u in range(16):
            for h in range(2):
                s_ref[h, pl.ds(pl.multiple_of((i * 16 + u) * BOX + 64, 8), 8), :] = blank[:8]

    step = 32
    for q in range(PIECES):

        @pl.loop(q * share // 4, (q + 1) * share // 4)
        def _(i):
            for u in range(4):
                o = i * 4 + u
                f_ref[pl.ds(pl.multiple_of(o * PER, PER), PER), :] = r_in[
                    o, 0:PER, :
                ].astype(F32)

        @pl.loop(q * sticks // PIECES // step, (q + 1) * sticks // PIECES // step)
        def _(i):
            for u in range(step):
                c = cell_ref[i * step + u]
                g_ref[pl.ds(pl.multiple_of(4 * c, 4), 4), :] = f_ref[
                    pl.ds(pl.multiple_of(i * 4 * step, 4 * step) + 4 * u, 4), :
                ]

    for copy in fixed:
        copy.wait()
    turn = 13

    @pl.loop(0, SIDE // turn)
    def _(i):
        xs = []
        for u in range(turn):
            r0 = (i * turn + u) * 4 * BOX
            halves = [
                jnp.concatenate(
                    [g_ref[pl.ds(r0 + 2 * h + p, BOX, stride=4), :] for p in range(2)], axis=0
                )
                for h in range(2)
            ]
            xs.append(jnp.concatenate(halves, axis=1).astype(BF))
        for u in range(turn):
            m = jnp.dot(ey_ref[...], xs[u], preferred_element_type=F32)
            for h in range(2):
                s_ref[h, pl.ds(i * turn + u, 2 * NR, stride=BOX), :] = m[
                    :, h * LANES : (h + 1) * LANES
                ]

    lane = lax.broadcasted_iota(jnp.int32, (NR, NR), 1)
    v = v_ref[...]
    batch = 16

    @pl.loop(0, NR // batch)
    def _(i):
        xs = []
        for u in range(batch):
            rows = pl.ds(pl.multiple_of((i * batch + u) * tall, 8), tall)
            xs.append(jnp.concatenate([s_ref[h, rows, :].astype(BF) for h in range(2)], axis=1))
        for u in range(batch):
            psi = jnp.dot(ex_ref[...], xs[u], preferred_element_type=F32)
            column = jnp.sum(
                jnp.where(lane == i * batch + u, v, 0.0), axis=1, keepdims=True
            )
            vv = jnp.broadcast_to(column, (NR, 2 * LANES))
            w_ref[u] = (psi * jnp.concatenate([vv, vv], axis=0)).astype(BF)
        for u in range(batch):
            m = jnp.dot(ix_ref[...], w_ref[u], preferred_element_type=F32)
            rows = pl.ds(pl.multiple_of((i * batch + u) * tall, 8), tall)
            for h in range(2):
                s_ref[h, rows, :] = m[:, h * LANES : (h + 1) * LANES]

    @pl.loop(0, SIDE // turn)
    def _(i):
        xs = []
        for u in range(turn):
            rows = pl.ds(i * turn + u, 2 * NR, stride=BOX)
            xs.append(jnp.concatenate([s_ref[h, rows, :].astype(BF) for h in range(2)], axis=1))
        for u in range(turn):
            m = jnp.dot(iy_ref[...], xs[u], preferred_element_type=F32)
            r0 = (i * turn + u) * 4 * BOX
            for h in range(2):
                for p in range(2):
                    g_ref[pl.ds(r0 + 2 * h + p, BOX, stride=4), :] = m[
                        p * BOX : (p + 1) * BOX, h * LANES : (h + 1) * LANES
                    ]

    for q in range(PIECES):

        @pl.loop(q * sticks // PIECES // step, (q + 1) * sticks // PIECES // step)
        def _(i):
            for u in range(step):
                c = cell_ref[i * step + u]
                f_ref[pl.ds(pl.multiple_of(i * 4 * step, 4 * step) + 4 * u, 4), :] = g_ref[
                    pl.ds(pl.multiple_of(4 * c, 4), 4), :
                ]

        @pl.loop(q * share // 4, (q + 1) * share // 4)
        def _(i):
            for u in range(4):
                o = i * 4 + u
                o_ref[o] = f_ref[pl.ds(pl.multiple_of(o * PER, PER), PER), :].astype(BF)


def plane_pass(cells, received, volume, tabs):
    owners = received.shape[0]
    return pl.pallas_call(
        plane_kernel,
        out_shape=jax.ShapeDtypeStruct((owners, PER, LANES), BF),
        in_specs=[SMEM, VMEM] + [HBM] * 5,
        out_specs=VMEM,
        scratch_shapes=[
            pltpu.VMEM(volume.shape, F32),
            *[pltpu.VMEM(t.shape, BF) for t in tabs],
            pltpu.VMEM((owners * PER, LANES), F32),
            pltpu.VMEM((SIDE * BOX * 4, LANES), F32),
            pltpu.VMEM((2, 2 * NR * BOX, LANES), F32),
            pltpu.VMEM((16, 2 * NR, 2 * LANES), BF),
            pltpu.SemaphoreType.DMA((5,)),
        ],
        compiler_params=pltpu.CompilerParams(vmem_limit_bytes=42 << 20),
        cost_estimate=pl.CostEstimate(
            flops=2 * 77000 * 256 * 256, bytes_accessed=6 << 20, transcendentals=0
        ),
        name="plane",
    )(cells, received, volume, *tabs)


def finish_kernel(r_ref, place_ref, i_ref, o_hbm, t_ref, sp_ref, out_ref, sem):
    place = place_ref[...]
    count = place.shape[1]
    spot = ((place >> 7) * BOX + ((place + HALF) & (NR - 1))).astype(F32)
    across = lax.broadcasted_iota(jnp.int32, (count, count), 1)
    down = lax.broadcasted_iota(jnp.int32, (count, count), 0)
    row = jnp.sum(jnp.where(across == down, spot, 0.0), axis=1, keepdims=True).astype(jnp.int32)
    at = lax.broadcasted_iota(jnp.int32, (count, SLOT * BOX), 1)
    select = jnp.where(at == row, 1.0 / NR**3, 0.0).astype(BF)

    @pl.loop(0, NR // 4)
    def _(i):
        for u in range(4):
            k = i * 4 + u
            t_ref[pl.ds(pl.multiple_of(k * PER, PER), PER), :] = r_ref[k].astype(F32)

    for s in range(SLOT):
        halves = [
            jnp.concatenate(
                [t_ref[pl.ds(4 * s + 2 * h + p, NR, stride=PER), :] for p in range(2)], axis=0
            )
            for h in range(2)
        ]
        x = jnp.concatenate(halves, axis=1).astype(BF)
        m = jnp.dot(i_ref[...], x, preferred_element_type=F32)
        for p in range(2):
            sp_ref[p, s * BOX : (s + 1) * BOX, :] = m[p * BOX : (p + 1) * BOX]
    sends = []
    for p in range(2):
        out_ref[p] = jnp.dot(select, sp_ref[p].astype(BF), preferred_element_type=F32)
        sends.append(pltpu.make_async_copy(out_ref.at[p], o_hbm.at[p], sem.at[p]))
        sends[p].start()
    for copy in sends:
        copy.wait()


def finish(returned, place, behind_z):
    out = jax.ShapeDtypeStruct((2, place.shape[1], 2 * LANES), F32)
    return pl.pallas_call(
        finish_kernel,
        out_shape=out,
        in_specs=[VMEM] * 3,
        out_specs=HBM,
        scratch_shapes=[
            pltpu.VMEM((NR * PER, LANES), F32),
            pltpu.VMEM((2, SLOT * BOX, 2 * LANES), F32),
            pltpu.VMEM(out.shape, F32),
            pltpu.SemaphoreType.DMA((2,)),
        ],
        compiler_params=pltpu.CompilerParams(vmem_limit_bytes=24 << 20),
        cost_estimate=pl.CostEstimate(
            flops=2 * (2304 + 2560) * 256 * 256, bytes_accessed=3 << 20, transcendentals=0
        ),
        name="finish",
    )(returned, place, behind_z)


def exchange(value):
    return lax.all_to_all(value, TG_PW, split_axis=0, concat_axis=0, tiled=True)


def body(coeffs, g_place, stick_column, potential):
    ahead_x, behind_x, behind_y, ahead_y = tables()
    place = g_place.reshape(1, -1)
    sent = spread(coeffs, place, stick_column, ahead_x)
    got = exchange(sent)
    column = got[:, PER, : 2 * SLOT].astype(F32).astype(jnp.int32)
    cells = (column[:, :SLOT] * BOX + column[:, SLOT:]).reshape(-1)
    volume = potential.reshape(NR, NR)
    done = plane_pass(cells, got, volume, (ahead_y, ahead_x, behind_x, behind_y))
    return finish(exchange(done), place, behind_x)


def solution(mesh):
    torus = Mesh(mesh.devices.reshape(mesh.shape["tg"], 4, 4, 4), ("tg", "pw_0", "pw_1", "pw_2"))
    return jax.shard_map(
        body,
        mesh=torus,
        in_specs=(P(None, TG_PW, None), P(TG_PW), P(TG_PW), P(None, None, TG_PW)),
        out_specs=P(None, TG_PW, None),
        check_vma=False,
    )
```

```python
import functools

import numpy as np
import jax
import jax.numpy as jnp
from jax import lax
from jax.experimental import pallas as pl
from jax.experimental.pallas import tpu as pltpu
from jax.sharding import Mesh
from jax.sharding import PartitionSpec as P

NR = 128
HALF = 32
BOX = 72
SIDE = 65
STEP = 73
SLOT = 16
LANES = 128
PER = 4 * SLOT
WIDE = PER + 1
PIECES = 4
TG_PW = ("tg", "pw_0", "pw_1", "pw_2")
BF = jnp.bfloat16
F32 = jnp.float32
VMEM = pl.BlockSpec(memory_space=pltpu.VMEM)
HBM = pl.BlockSpec(memory_space=pltpu.HBM)
SMEM = pl.BlockSpec(memory_space=pltpu.SMEM)


def complex_table(rows, cols, sign, keep_rows, keep_cols):
    angle = 2.0 * np.pi / NR * (np.outer(rows, cols) % NR)
    keep = keep_rows[:, None] * keep_cols[None, :]
    c = np.cos(angle) * keep
    s = sign * np.sin(angle) * keep
    return np.stack([np.stack([c, -s], 1), np.stack([s, c], 1)]).astype(np.float32)


def tables():
    full = np.arange(NR)
    box = np.arange(BOX) - HALF
    keep_box = (np.arange(BOX) <= 2 * HALF).astype(np.float32)
    keep_all = np.ones(NR, np.float32)
    ahead = complex_table(full, box, 1.0, keep_all, keep_box)
    behind = complex_table(box, full, -1.0, keep_box, keep_all)
    wide, tall = 2 * NR, 2 * BOX
    ahead_x = ahead.reshape(wide, tall)
    behind_x = behind.reshape(tall, wide)
    behind_y = behind.transpose(0, 1, 3, 2).reshape(tall, wide)
    ahead_y = ahead.transpose(1, 0, 2, 3).reshape(wide, tall)
    return [jnp.asarray(t, BF) for t in (ahead_x, behind_x, behind_y, ahead_y)]


def spread_kernel(
    c_hbm, place_hbm, column_ref, e_hbm, o_hbm, c_ref, place_ref, e_ref, t_ref, o_ref, sem
):
    first = pltpu.make_async_copy(place_hbm, place_ref, sem.at[PIECES])
    first.start()
    copies = [pltpu.make_async_copy(c_hbm.at[p], c_ref.at[p], sem.at[p]) for p in range(2)]
    copies.append(pltpu.make_async_copy(e_hbm, e_ref, sem.at[2]))
    for copy in copies:
        copy.start()
    first.wait()
    place = place_ref[...]
    row = (place >> 7) * BOX + ((place + HALF) & (NR - 1))
    at = lax.broadcasted_iota(jnp.int32, (SLOT * BOX, place.shape[1]), 0)
    select = jnp.where(at == row, 1.0, 0.0).astype(BF)
    lane = lax.broadcasted_iota(jnp.int32, (8, LANES), 1)
    info = jnp.zeros((8, LANES), jnp.int32)
    for s in range(SLOT):
        column = column_ref[s]
        info = jnp.where(lane == s, ((column >> 7) + HALF) & (NR - 1), info)
        info = jnp.where(lane == SLOT + s, (column + HALF) & (NR - 1), info)
    info = info.astype(F32).astype(BF)
    for copy in copies:
        copy.wait()
    both = jnp.concatenate([c_ref[p].astype(BF) for p in range(2)], axis=1)
    placed = jnp.dot(select, both, preferred_element_type=F32)
    xs = []
    for s in range(SLOT):
        rows = placed[s * BOX : (s + 1) * BOX]
        xs.append(
            jnp.concatenate([rows[:, : 2 * LANES], rows[:, 2 * LANES :]], axis=0).astype(BF)
        )
    for s in range(SLOT):
        m = jnp.dot(e_ref[...], xs[s], preferred_element_type=F32)
        for h in range(2):
            for p in range(2):
                t_ref[pl.ds(4 * s + 2 * h + p, NR, stride=WIDE), :] = m[
                    p * NR : (p + 1) * NR, h * LANES : (h + 1) * LANES
                ]
    share = NR // PIECES
    sends = []
    for q in range(PIECES):

        @pl.loop(q * share // 8, (q + 1) * share // 8)
        def _(i):
            for u in range(8):
                k = i * 8 + u
                o_ref[k, 0:PER, :] = t_ref[pl.ds(k * WIDE, PER), :].astype(BF)
                o_ref[k, PER : PER + 8, :] = info

        part = pl.ds(q * share, share)
        sends.append(pltpu.make_async_copy(o_ref.at[part], o_hbm.at[part], sem.at[q]))
        sends[q].start()
    for copy in sends:
        copy.wait()


def spread(coeffs, place, columns, ahead_z):
    out = jax.ShapeDtypeStruct((NR, PER + 8, LANES), BF)
    return pl.pallas_call(
        spread_kernel,
        out_shape=out,
        in_specs=[HBM, HBM, SMEM, HBM],
        out_specs=HBM,
        scratch_shapes=[
            pltpu.VMEM(coeffs.shape, F32),
            pltpu.VMEM(place.shape, jnp.int32),
            pltpu.VMEM(ahead_z.shape, BF),
            pltpu.VMEM((NR * WIDE, LANES), F32),
            pltpu.VMEM(out.shape, BF),
            pltpu.SemaphoreType.DMA((PIECES + 1,)),
        ],
        compiler_params=pltpu.CompilerParams(vmem_limit_bytes=62 << 20),
        cost_estimate=pl.CostEstimate(
            flops=2 * (2304 + 4096) * 256 * 256, bytes_accessed=3 << 20, transcendentals=0
        ),
        name="spread",
    )(coeffs, place, columns, ahead_z)


def plane_kernel(
    cell_ref, r_in, v_hbm, ey_hbm, ex_hbm, ix_hbm, iy_hbm, o_ref,
    v_ref, ey_ref, ex_ref, ix_ref, iy_ref, f_ref, g_ref, s_ref, w_ref, sem,
):
    owners = o_ref.shape[0]
    sticks = owners * SLOT
    share = owners // PIECES
    fixed = [
        pltpu.make_async_copy(src, dst, sem.at[n])
        for n, (src, dst) in enumerate(
            [(ey_hbm, ey_ref), (v_hbm, v_ref), (ex_hbm, ex_ref), (ix_hbm, ix_ref), (iy_hbm, iy_ref)]
        )
    ]
    for copy in fixed:
        copy.start()
    blank = jnp.zeros((4 * BOX, LANES), F32)

    @pl.loop(0, SIDE)
    def _(x):
        g_ref[pl.ds(pl.multiple_of(x * 4 * BOX, 8), 4 * BOX), :] = blank

    @pl.loop(0, NR // 8)
    def _(i):
        for u in range(16):
            for h in range(2):
                s_ref[h, pl.ds((i * 16 + u) * STEP + 64, 8), :] = blank[:8]

    step = 32
    for q in range(PIECES):

        @pl.loop(q * share // 4, (q + 1) * share // 4)
        def _(i):
            for u in range(4):
                o = i * 4 + u
                f_ref[pl.ds(pl.multiple_of(o * PER, PER), PER), :] = r_in[
                    o, 0:PER, :
                ].astype(F32)

        @pl.loop(q * sticks // PIECES // step, (q + 1) * sticks // PIECES // step)
        def _(i):
            for u in range(step):
                c = cell_ref[i * step + u]
                g_ref[pl.ds(pl.multiple_of(4 * c, 4), 4), :] = f_ref[
                    pl.ds(pl.multiple_of(i * 4 * step, 4 * step) + 4 * u, 4), :
                ]

    for copy in fixed:
        copy.wait()
    turn = 13

    @pl.loop(0, SIDE // turn)
    def _(i):
        xs = []
        for u in range(turn):
            r0 = (i * turn + u) * 4 * BOX
            halves = [
                jnp.concatenate(
                    [g_ref[pl.ds(r0 + 2 * h + p, BOX, stride=4), :] for p in range(2)], axis=0
                )
                for h in range(2)
            ]
            xs.append(jnp.concatenate(halves, axis=1).astype(BF))
        for u in range(turn):
            m = jnp.dot(ey_ref[...], xs[u], preferred_element_type=F32)
            for h in range(2):
                s_ref[h, pl.ds(i * turn + u, 2 * NR, stride=STEP), :] = m[
                    :, h * LANES : (h + 1) * LANES
                ]

    lane = lax.broadcasted_iota(jnp.int32, (NR, NR), 1)
    v = v_ref[...]
    batch = 16

    @pl.loop(0, NR // batch)
    def _(i):
        xs = []
        for u in range(batch):
            r0 = (i * batch + u) * 2 * STEP
            halves = [
                jnp.concatenate(
                    [s_ref[h, pl.ds(r0 + p * STEP, BOX), :] for p in range(2)], axis=0
                )
                for h in range(2)
            ]
            xs.append(jnp.concatenate(halves, axis=1).astype(BF))
        for u in range(batch):
            psi = jnp.dot(ex_ref[...], xs[u], preferred_element_type=F32)
            column = jnp.sum(
                jnp.where(lane == i * batch + u, v, 0.0), axis=1, keepdims=True
            )
            vv = jnp.broadcast_to(column, (NR, 2 * LANES))
            w_ref[u] = (psi * jnp.concatenate([vv, vv], axis=0)).astype(BF)
        for u in range(batch):
            m = jnp.dot(ix_ref[...], w_ref[u], preferred_element_type=F32)
            r0 = (i * batch + u) * 2 * STEP
            for h in range(2):
                for p in range(2):
                    s_ref[h, pl.ds(r0 + p * STEP, BOX), :] = m[
                        p * BOX : (p + 1) * BOX, h * LANES : (h + 1) * LANES
                    ]

    @pl.loop(0, SIDE // turn)
    def _(i):
        xs = []
        for u in range(turn):
            rows = pl.ds(i * turn + u, 2 * NR, stride=STEP)
            xs.append(jnp.concatenate([s_ref[h, rows, :].astype(BF) for h in range(2)], axis=1))
        for u in range(turn):
            m = jnp.dot(iy_ref[...], xs[u], preferred_element_type=F32)
            r0 = (i * turn + u) * 4 * BOX
            for h in range(2):
                for p in range(2):
                    g_ref[pl.ds(r0 + 2 * h + p, BOX, stride=4), :] = m[
                        p * BOX : (p + 1) * BOX, h * LANES : (h + 1) * LANES
                    ]

    for q in range(PIECES):

        @pl.loop(q * sticks // PIECES // step, (q + 1) * sticks // PIECES // step)
        def _(i):
            for u in range(step):
                c = cell_ref[i * step + u]
                f_ref[pl.ds(pl.multiple_of(i * 4 * step, 4 * step) + 4 * u, 4), :] = g_ref[
                    pl.ds(pl.multiple_of(4 * c, 4), 4), :
                ]

        @pl.loop(q * share // 4, (q + 1) * share // 4)
        def _(i):
            for u in range(4):
                o = i * 4 + u
                o_ref[o] = f_ref[pl.ds(pl.multiple_of(o * PER, PER), PER), :].astype(BF)


def plane_pass(cells, received, volume, tabs):
    owners = received.shape[0]
    return pl.pallas_call(
        plane_kernel,
        out_shape=jax.ShapeDtypeStruct((owners, PER, LANES), BF),
        in_specs=[SMEM, VMEM] + [HBM] * 5,
        out_specs=VMEM,
        scratch_shapes=[
            pltpu.VMEM(volume.shape, F32),
            *[pltpu.VMEM(t.shape, BF) for t in tabs],
            pltpu.VMEM((owners * PER, LANES), F32),
            pltpu.VMEM((SIDE * BOX * 4, LANES), F32),
            pltpu.VMEM((2, 2 * NR * STEP, LANES), F32),
            pltpu.VMEM((16, 2 * NR, 2 * LANES), BF),
            pltpu.SemaphoreType.DMA((5,)),
        ],
        compiler_params=pltpu.CompilerParams(vmem_limit_bytes=42 << 20),
        cost_estimate=pl.CostEstimate(
            flops=2 * 77000 * 256 * 256, bytes_accessed=6 << 20, transcendentals=0
        ),
        name="plane",
    )(cells, received, volume, *tabs)


def finish_kernel(r_ref, place_ref, i_ref, o_hbm, t_ref, sp_ref, out_ref, sem):
    place = place_ref[...]
    count = place.shape[1]
    spot = ((place >> 7) * BOX + ((place + HALF) & (NR - 1))).astype(F32)
    across = lax.broadcasted_iota(jnp.int32, (count, count), 1)
    down = lax.broadcasted_iota(jnp.int32, (count, count), 0)
    row = jnp.sum(jnp.where(across == down, spot, 0.0), axis=1, keepdims=True).astype(jnp.int32)
    at = lax.broadcasted_iota(jnp.int32, (count, SLOT * BOX), 1)
    select = jnp.where(at == row, 1.0 / NR**3, 0.0).astype(BF)

    @pl.loop(0, NR // 8)
    def _(i):
        for u in range(8):
            k = i * 8 + u
            t_ref[pl.ds(k * WIDE, PER), :] = r_ref[k].astype(F32)

    for s in range(SLOT):
        halves = [
            jnp.concatenate(
                [t_ref[pl.ds(4 * s + 2 * h + p, NR, stride=WIDE), :] for p in range(2)], axis=0
            )
            for h in range(2)
        ]
        x = jnp.concatenate(halves, axis=1).astype(BF)
        m = jnp.dot(i_ref[...], x, preferred_element_type=F32)
        for p in range(2):
            sp_ref[p, s * BOX : (s + 1) * BOX, :] = m[p * BOX : (p + 1) * BOX]
    sends = []
    for p in range(2):
        out_ref[p] = jnp.dot(select, sp_ref[p].astype(BF), preferred_element_type=F32)
        sends.append(pltpu.make_async_copy(out_ref.at[p], o_hbm.at[p], sem.at[p]))
        sends[p].start()
    for copy in sends:
        copy.wait()


def finish(returned, place, behind_z):
    out = jax.ShapeDtypeStruct((2, place.shape[1], 2 * LANES), F32)
    return pl.pallas_call(
        finish_kernel,
        out_shape=out,
        in_specs=[VMEM] * 3,
        out_specs=HBM,
        scratch_shapes=[
            pltpu.VMEM((NR * WIDE, LANES), F32),
            pltpu.VMEM((2, SLOT * BOX, 2 * LANES), F32),
            pltpu.VMEM(out.shape, F32),
            pltpu.SemaphoreType.DMA((2,)),
        ],
        compiler_params=pltpu.CompilerParams(vmem_limit_bytes=24 << 20),
        cost_estimate=pl.CostEstimate(
            flops=2 * (2304 + 2560) * 256 * 256, bytes_accessed=3 << 20, transcendentals=0
        ),
        name="finish",
    )(returned, place, behind_z)


def exchange(value):
    return lax.all_to_all(value, TG_PW, split_axis=0, concat_axis=0, tiled=True)


def body(coeffs, g_place, stick_column, potential):
    ahead_x, behind_x, behind_y, ahead_y = tables()
    place = g_place.reshape(1, -1)
    sent = spread(coeffs, place, stick_column, ahead_x)
    got = exchange(sent)
    column = got[:, PER, : 2 * SLOT].astype(F32).astype(jnp.int32)
    cells = (column[:, :SLOT] * BOX + column[:, SLOT:]).reshape(-1)
    volume = potential.reshape(NR, NR)
    done = plane_pass(cells, got, volume, (ahead_y, ahead_x, behind_x, behind_y))
    return finish(exchange(done), place, behind_x)


def solution(mesh):
    torus = Mesh(mesh.devices.reshape(mesh.shape["tg"], 4, 4, 4), ("tg", "pw_0", "pw_1", "pw_2"))
    return jax.shard_map(
        body,
        mesh=torus,
        in_specs=(P(None, TG_PW, None), P(TG_PW), P(TG_PW), P(None, None, TG_PW)),
        out_specs=P(None, TG_PW, None),
        check_vma=False,
    )
```

```python
import functools

import numpy as np
import jax
import jax.numpy as jnp
from jax import lax
from jax.experimental import pallas as pl
from jax.experimental.pallas import tpu as pltpu
from jax.sharding import Mesh
from jax.sharding import PartitionSpec as P

NR = 128
HALF = 32
BOX = 72
SIDE = 65
STEP = 73
SLOT = 16
LANES = 128
PER = 4 * SLOT
WIDE = PER + 1
PIECES = 4
TG_PW = ("tg", "pw_0", "pw_1", "pw_2")
BF = jnp.bfloat16
F32 = jnp.float32
VMEM = pl.BlockSpec(memory_space=pltpu.VMEM)
HBM = pl.BlockSpec(memory_space=pltpu.HBM)
SMEM = pl.BlockSpec(memory_space=pltpu.SMEM)


def complex_table(rows, cols, sign, keep_rows, keep_cols):
    angle = 2.0 * np.pi / NR * (np.outer(rows, cols) % NR)
    keep = keep_rows[:, None] * keep_cols[None, :]
    c = np.cos(angle) * keep
    s = sign * np.sin(angle) * keep
    return np.stack([np.stack([c, -s], 1), np.stack([s, c], 1)]).astype(np.float32)


def tables():
    full = np.arange(NR)
    box = np.arange(BOX) - HALF
    keep_box = (np.arange(BOX) <= 2 * HALF).astype(np.float32)
    keep_all = np.ones(NR, np.float32)
    ahead = complex_table(full, box, 1.0, keep_all, keep_box)
    behind = complex_table(box, full, -1.0, keep_box, keep_all)
    wide, tall = 2 * NR, 2 * BOX
    ahead_x = ahead.reshape(wide, tall)
    behind_x = behind.reshape(tall, wide)
    behind_y = behind.transpose(0, 1, 3, 2).reshape(tall, wide)
    ahead_y = ahead.transpose(1, 0, 2, 3).reshape(wide, tall)
    return [jnp.asarray(t, BF) for t in (ahead_x, behind_x, behind_y, ahead_y)]


def spread_kernel(
    c_hbm, place_hbm, column_ref, e_hbm, o_hbm, c_ref, place_ref, e_ref, t_ref, o_ref, sem
):
    first = pltpu.make_async_copy(place_hbm, place_ref, sem.at[PIECES])
    first.start()
    copies = [pltpu.make_async_copy(c_hbm.at[p], c_ref.at[p], sem.at[p]) for p in range(2)]
    copies.append(pltpu.make_async_copy(e_hbm, e_ref, sem.at[2]))
    for copy in copies:
        copy.start()
    first.wait()
    place = place_ref[...]
    row = (place >> 7) * BOX + ((place + HALF) & (NR - 1))
    at = lax.broadcasted_iota(jnp.int32, (SLOT * BOX, place.shape[1]), 0)
    select = jnp.where(at == row, 1.0, 0.0).astype(BF)
    lane = lax.broadcasted_iota(jnp.int32, (8, LANES), 1)
    info = jnp.zeros((8, LANES), jnp.int32)
    for s in range(SLOT):
        column = column_ref[s]
        info = jnp.where(lane == s, ((column >> 7) + HALF) & (NR - 1), info)
        info = jnp.where(lane == SLOT + s, (column + HALF) & (NR - 1), info)
    info = info.astype(F32).astype(BF)
    for copy in copies:
        copy.wait()
    both = jnp.concatenate([c_ref[p].astype(BF) for p in range(2)], axis=1)
    placed = jnp.dot(select, both, preferred_element_type=F32)
    xs = []
    for s in range(SLOT):
        rows = placed[s * BOX : (s + 1) * BOX]
        xs.append(
            jnp.concatenate([rows[:, : 2 * LANES], rows[:, 2 * LANES :]], axis=0).astype(BF)
        )
    for s in range(SLOT):
        m = jnp.dot(e_ref[...], xs[s], preferred_element_type=F32)
        for h in range(2):
            for p in range(2):
                t_ref[pl.ds(4 * s + 2 * h + p, NR, stride=WIDE), :] = m[
                    p * NR : (p + 1) * NR, h * LANES : (h + 1) * LANES
                ]
    share = NR // PIECES
    sends = []
    for q in range(PIECES):

        @pl.loop(q * share // 8, (q + 1) * share // 8)
        def _(i):
            for u in range(8):
                k = i * 8 + u
                o_ref[k, 0:PER, :] = t_ref[pl.ds(k * WIDE, PER), :].astype(BF)
                o_ref[k, PER : PER + 8, :] = info

        part = pl.ds(q * share, share)
        sends.append(pltpu.make_async_copy(o_ref.at[part], o_hbm.at[part], sem.at[q]))
        sends[q].start()
    for copy in sends:
        copy.wait()


def spread(coeffs, place, columns, ahead_z):
    out = jax.ShapeDtypeStruct((NR, PER + 8, LANES), BF)
    return pl.pallas_call(
        spread_kernel,
        out_shape=out,
        in_specs=[HBM, HBM, SMEM, HBM],
        out_specs=HBM,
        scratch_shapes=[
            pltpu.VMEM(coeffs.shape, F32),
            pltpu.VMEM(place.shape, jnp.int32),
            pltpu.VMEM(ahead_z.shape, BF),
            pltpu.VMEM((NR * WIDE, LANES), F32),
            pltpu.VMEM(out.shape, BF),
            pltpu.SemaphoreType.DMA((PIECES + 1,)),
        ],
        compiler_params=pltpu.CompilerParams(vmem_limit_bytes=62 << 20),
        cost_estimate=pl.CostEstimate(
            flops=2 * (2304 + 4096) * 256 * 256, bytes_accessed=3 << 20, transcendentals=0
        ),
        name="spread",
    )(coeffs, place, columns, ahead_z)


def plane_kernel(
    cell_ref, r_in, v_hbm, ey_hbm, ex_hbm, ix_hbm, iy_hbm, o_ref,
    v_ref, ey_ref, ex_ref, ix_ref, iy_ref, f_ref, g_ref, s_ref, w_ref, sem,
):
    owners = o_ref.shape[0]
    sticks = owners * SLOT
    share = owners // PIECES
    fixed = [
        pltpu.make_async_copy(src, dst, sem.at[n])
        for n, (src, dst) in enumerate(
            [(ey_hbm, ey_ref), (v_hbm, v_ref), (ex_hbm, ex_ref), (ix_hbm, ix_ref), (iy_hbm, iy_ref)]
        )
    ]
    for copy in fixed:
        copy.start()
    blank = jnp.zeros((4 * BOX, LANES), F32)

    @pl.loop(0, SIDE)
    def _(x):
        g_ref[pl.ds(pl.multiple_of(x * 4 * BOX, 8), 4 * BOX), :] = blank

    @pl.loop(0, NR // 8)
    def _(i):
        for u in range(16):
            for h in range(2):
                s_ref[h, pl.ds((i * 16 + u) * STEP + 64, 8), :] = blank[:8]

    step = 128
    for q in range(PIECES):

        @pl.loop(q * share // 16, (q + 1) * share // 16)
        def _(i):
            for u in range(16):
                o = i * 16 + u
                f_ref[pl.ds(pl.multiple_of(o * PER, PER), PER), :] = r_in[
                    o, 0:PER, :
                ].astype(F32)

        @pl.loop(q * sticks // PIECES // step, (q + 1) * sticks // PIECES // step)
        def _(i):
            for u in range(step):
                c = cell_ref[i * step + u]
                g_ref[pl.ds(pl.multiple_of(4 * c, 4), 4), :] = f_ref[
                    pl.ds(pl.multiple_of(i * 4 * step, 4 * step) + 4 * u, 4), :
                ]

    for copy in fixed:
        copy.wait()
    turn = SIDE

    @pl.loop(0, SIDE // turn)
    def _(i):
        xs = []
        for u in range(turn):
            r0 = (i * turn + u) * 4 * BOX
            halves = [
                jnp.concatenate(
                    [g_ref[pl.ds(r0 + 2 * h + p, BOX, stride=4), :] for p in range(2)], axis=0
                )
                for h in range(2)
            ]
            xs.append(jnp.concatenate(halves, axis=1).astype(BF))
        for u in range(turn):
            m = jnp.dot(ey_ref[...], xs[u], preferred_element_type=F32)
            for h in range(2):
                s_ref[h, pl.ds(i * turn + u, 2 * NR, stride=STEP), :] = m[
                    :, h * LANES : (h + 1) * LANES
                ]

    lane = lax.broadcasted_iota(jnp.int32, (NR, NR), 1)
    v = v_ref[...]
    batch = 32

    @pl.loop(0, NR // batch)
    def _(i):
        xs = []
        for u in range(batch):
            r0 = (i * batch + u) * 2 * STEP
            halves = [
                jnp.concatenate(
                    [s_ref[h, pl.ds(r0 + p * STEP, BOX), :] for p in range(2)], axis=0
                )
                for h in range(2)
            ]
            xs.append(jnp.concatenate(halves, axis=1).astype(BF))
        for u in range(batch):
            psi = jnp.dot(ex_ref[...], xs[u], preferred_element_type=F32)
            column = jnp.sum(
                jnp.where(lane == i * batch + u, v, 0.0), axis=1, keepdims=True
            )
            vv = jnp.broadcast_to(column, (NR, 2 * LANES))
            w_ref[u] = (psi * jnp.concatenate([vv, vv], axis=0)).astype(BF)
        for u in range(batch):
            m = jnp.dot(ix_ref[...], w_ref[u], preferred_element_type=F32)
            r0 = (i * batch + u) * 2 * STEP
            for h in range(2):
                for p in range(2):
                    s_ref[h, pl.ds(r0 + p * STEP, BOX), :] = m[
                        p * BOX : (p + 1) * BOX, h * LANES : (h + 1) * LANES
                    ]

    @pl.loop(0, SIDE // turn)
    def _(i):
        xs = []
        for u in range(turn):
            rows = pl.ds(i * turn + u, 2 * NR, stride=STEP)
            xs.append(jnp.concatenate([s_ref[h, rows, :].astype(BF) for h in range(2)], axis=1))
        for u in range(turn):
            m = jnp.dot(iy_ref[...], xs[u], preferred_element_type=F32)
            r0 = (i * turn + u) * 4 * BOX
            for h in range(2):
                for p in range(2):
                    g_ref[pl.ds(r0 + 2 * h + p, BOX, stride=4), :] = m[
                        p * BOX : (p + 1) * BOX, h * LANES : (h + 1) * LANES
                    ]

    for q in range(PIECES):

        @pl.loop(q * sticks // PIECES // step, (q + 1) * sticks // PIECES // step)
        def _(i):
            for u in range(step):
                c = cell_ref[i * step + u]
                f_ref[pl.ds(pl.multiple_of(i * 4 * step, 4 * step) + 4 * u, 4), :] = g_ref[
                    pl.ds(pl.multiple_of(4 * c, 4), 4), :
                ]

        @pl.loop(q * share // 16, (q + 1) * share // 16)
        def _(i):
            for u in range(16):
                o = i * 16 + u
                o_ref[o] = f_ref[pl.ds(pl.multiple_of(o * PER, PER), PER), :].astype(BF)


def plane_pass(cells, received, volume, tabs):
    owners = received.shape[0]
    return pl.pallas_call(
        plane_kernel,
        out_shape=jax.ShapeDtypeStruct((owners, PER, LANES), BF),
        in_specs=[SMEM, VMEM] + [HBM] * 5,
        out_specs=VMEM,
        scratch_shapes=[
            pltpu.VMEM(volume.shape, F32),
            *[pltpu.VMEM(t.shape, BF) for t in tabs],
            pltpu.VMEM((owners * PER, LANES), F32),
            pltpu.VMEM((SIDE * BOX * 4, LANES), F32),
            pltpu.VMEM((2, 2 * NR * STEP, LANES), F32),
            pltpu.VMEM((32, 2 * NR, 2 * LANES), BF),
            pltpu.SemaphoreType.DMA((5,)),
        ],
        compiler_params=pltpu.CompilerParams(vmem_limit_bytes=48 << 20),
        cost_estimate=pl.CostEstimate(
            flops=2 * 77000 * 256 * 256, bytes_accessed=6 << 20, transcendentals=0
        ),
        name="plane",
    )(cells, received, volume, *tabs)


def finish_kernel(r_ref, place_ref, i_ref, o_hbm, t_ref, sp_ref, out_ref, sem):
    place = place_ref[...]
    count = place.shape[1]
    spot = ((place >> 7) * BOX + ((place + HALF) & (NR - 1))).astype(F32)
    across = lax.broadcasted_iota(jnp.int32, (count, count), 1)
    down = lax.broadcasted_iota(jnp.int32, (count, count), 0)
    row = jnp.sum(jnp.where(across == down, spot, 0.0), axis=1, keepdims=True).astype(jnp.int32)
    at = lax.broadcasted_iota(jnp.int32, (count, SLOT * BOX), 1)
    select = jnp.where(at == row, 1.0 / NR**3, 0.0).astype(BF)

    @pl.loop(0, NR // 8)
    def _(i):
        for u in range(8):
            k = i * 8 + u
            t_ref[pl.ds(k * WIDE, PER), :] = r_ref[k].astype(F32)

    for s in range(SLOT):
        halves = [
            jnp.concatenate(
                [t_ref[pl.ds(4 * s + 2 * h + p, NR, stride=WIDE), :] for p in range(2)], axis=0
            )
            for h in range(2)
        ]
        x = jnp.concatenate(halves, axis=1).astype(BF)
        m = jnp.dot(i_ref[...], x, preferred_element_type=F32)
        for p in range(2):
            sp_ref[p, s * BOX : (s + 1) * BOX, :] = m[p * BOX : (p + 1) * BOX]
    sends = []
    for p in range(2):
        out_ref[p] = jnp.dot(select, sp_ref[p].astype(BF), preferred_element_type=F32)
        sends.append(pltpu.make_async_copy(out_ref.at[p], o_hbm.at[p], sem.at[p]))
        sends[p].start()
    for copy in sends:
        copy.wait()


def finish(returned, place, behind_z):
    out = jax.ShapeDtypeStruct((2, place.shape[1], 2 * LANES), F32)
    return pl.pallas_call(
        finish_kernel,
        out_shape=out,
        in_specs=[VMEM] * 3,
        out_specs=HBM,
        scratch_shapes=[
            pltpu.VMEM((NR * WIDE, LANES), F32),
            pltpu.VMEM((2, SLOT * BOX, 2 * LANES), F32),
            pltpu.VMEM(out.shape, F32),
            pltpu.SemaphoreType.DMA((2,)),
        ],
        compiler_params=pltpu.CompilerParams(vmem_limit_bytes=24 << 20),
        cost_estimate=pl.CostEstimate(
            flops=2 * (2304 + 2560) * 256 * 256, bytes_accessed=3 << 20, transcendentals=0
        ),
        name="finish",
    )(returned, place, behind_z)


def exchange(value):
    return lax.all_to_all(value, TG_PW, split_axis=0, concat_axis=0, tiled=True)


def body(coeffs, g_place, stick_column, potential):
    ahead_x, behind_x, behind_y, ahead_y = tables()
    place = g_place.reshape(1, -1)
    sent = spread(coeffs, place, stick_column, ahead_x)
    got = exchange(sent)
    column = got[:, PER, : 2 * SLOT].astype(F32).astype(jnp.int32)
    cells = (column[:, :SLOT] * BOX + column[:, SLOT:]).reshape(-1)
    volume = potential.reshape(NR, NR)
    done = plane_pass(cells, got, volume, (ahead_y, ahead_x, behind_x, behind_y))
    return finish(exchange(done), place, behind_x)


def solution(mesh):
    torus = Mesh(mesh.devices.reshape(mesh.shape["tg"], 4, 4, 4), ("tg", "pw_0", "pw_1", "pw_2"))
    return jax.shard_map(
        body,
        mesh=torus,
        in_specs=(P(None, TG_PW, None), P(TG_PW), P(TG_PW), P(None, None, TG_PW)),
        out_specs=P(None, TG_PW, None),
        check_vma=False,
    )
```

```python
import functools

import numpy as np
import jax
import jax.numpy as jnp
from jax import lax
from jax.experimental import pallas as pl
from jax.experimental.pallas import tpu as pltpu
from jax.sharding import Mesh
from jax.sharding import PartitionSpec as P

NR = 128
HALF = 32
BOX = 72
SIDE = 65
STEP = 73
SLOT = 16
LANES = 128
PER = 4 * SLOT
WIDE = PER + 1
PIECES = 8
TG_PW = ("tg", "pw_0", "pw_1", "pw_2")
BF = jnp.bfloat16
F32 = jnp.float32
VMEM = pl.BlockSpec(memory_space=pltpu.VMEM)
HBM = pl.BlockSpec(memory_space=pltpu.HBM)
SMEM = pl.BlockSpec(memory_space=pltpu.SMEM)


def complex_table(rows, cols, sign, keep_rows, keep_cols):
    angle = 2.0 * np.pi / NR * (np.outer(rows, cols) % NR)
    keep = keep_rows[:, None] * keep_cols[None, :]
    c = np.cos(angle) * keep
    s = sign * np.sin(angle) * keep
    return np.stack([np.stack([c, -s], 1), np.stack([s, c], 1)]).astype(np.float32)


def tables():
    full = np.arange(NR)
    box = np.arange(BOX) - HALF
    keep_box = (np.arange(BOX) <= 2 * HALF).astype(np.float32)
    keep_all = np.ones(NR, np.float32)
    ahead = complex_table(full, box, 1.0, keep_all, keep_box)
    behind = complex_table(box, full, -1.0, keep_box, keep_all)
    wide, tall = 2 * NR, 2 * BOX
    ahead_x = ahead.reshape(wide, tall)
    behind_x = behind.reshape(tall, wide)
    behind_y = behind.transpose(0, 1, 3, 2).reshape(tall, wide)
    ahead_y = ahead.transpose(1, 0, 2, 3).reshape(wide, tall)
    return [jnp.asarray(t, BF) for t in (ahead_x, behind_x, behind_y, ahead_y)]


def spread_kernel(
    c_hbm, place_hbm, column_ref, e_hbm, o_hbm, c_ref, place_ref, e_ref, t_ref, o_ref, sem
):
    first = pltpu.make_async_copy(place_hbm, place_ref, sem.at[PIECES])
    first.start()
    copies = [pltpu.make_async_copy(c_hbm.at[p], c_ref.at[p], sem.at[p]) for p in range(2)]
    copies.append(pltpu.make_async_copy(e_hbm, e_ref, sem.at[2]))
    for copy in copies:
        copy.start()
    first.wait()
    place = place_ref[...]
    row = (place >> 7) * BOX + ((place + HALF) & (NR - 1))
    at = lax.broadcasted_iota(jnp.int32, (SLOT * BOX, place.shape[1]), 0)
    select = jnp.where(at == row, 1.0, 0.0).astype(BF)
    lane = lax.broadcasted_iota(jnp.int32, (8, LANES), 1)
    info = jnp.zeros((8, LANES), jnp.int32)
    for s in range(SLOT):
        column = column_ref[s]
        info = jnp.where(lane == s, ((column >> 7) + HALF) & (NR - 1), info)
        info = jnp.where(lane == SLOT + s, (column + HALF) & (NR - 1), info)
    info = info.astype(F32).astype(BF)
    for copy in copies:
        copy.wait()
    both = jnp.concatenate([c_ref[p].astype(BF) for p in range(2)], axis=1)
    placed = jnp.dot(select, both, preferred_element_type=F32)
    xs = []
    for s in range(SLOT):
        rows = placed[s * BOX : (s + 1) * BOX]
        xs.append(
            jnp.concatenate([rows[:, : 2 * LANES], rows[:, 2 * LANES :]], axis=0).astype(BF)
        )
    for s in range(SLOT):
        m = jnp.dot(e_ref[...], xs[s], preferred_element_type=F32)
        for h in range(2):
            for p in range(2):
                t_ref[pl.ds(4 * s + 2 * h + p, NR, stride=WIDE), :] = m[
                    p * NR : (p + 1) * NR, h * LANES : (h + 1) * LANES
                ]
    share = NR // PIECES
    sends = []
    for q in range(PIECES):

        @pl.loop(q * share // 8, (q + 1) * share // 8)
        def _(i):
            for u in range(8):
                k = i * 8 + u
                o_ref[k, 0:PER, :] = t_ref[pl.ds(k * WIDE, PER), :].astype(BF)
                o_ref[k, PER : PER + 8, :] = info

        part = pl.ds(q * share, share)
        sends.append(pltpu.make_async_copy(o_ref.at[part], o_hbm.at[part], sem.at[q]))
        sends[q].start()
    for copy in sends:
        copy.wait()


def spread(coeffs, place, columns, ahead_z):
    out = jax.ShapeDtypeStruct((NR, PER + 8, LANES), BF)
    return pl.pallas_call(
        spread_kernel,
        out_shape=out,
        in_specs=[HBM, HBM, SMEM, HBM],
        out_specs=HBM,
        scratch_shapes=[
            pltpu.VMEM(coeffs.shape, F32),
            pltpu.VMEM(place.shape, jnp.int32),
            pltpu.VMEM(ahead_z.shape, BF),
            pltpu.VMEM((NR * WIDE, LANES), F32),
            pltpu.VMEM(out.shape, BF),
            pltpu.SemaphoreType.DMA((PIECES + 1,)),
        ],
        compiler_params=pltpu.CompilerParams(vmem_limit_bytes=62 << 20),
        cost_estimate=pl.CostEstimate(
            flops=2 * (2304 + 4096) * 256 * 256, bytes_accessed=3 << 20, transcendentals=0
        ),
        name="spread",
    )(coeffs, place, columns, ahead_z)


def plane_kernel(
    r_in, v_hbm, ey_hbm, ex_hbm, ix_hbm, iy_hbm, o_ref,
    v_ref, ey_ref, ex_ref, ix_ref, iy_ref, f_ref, g_ref, s_ref, w_ref, c_ref, cell_ref, sem,
):
    owners = o_ref.shape[0]
    sticks = owners * SLOT
    fixed = [
        pltpu.make_async_copy(src, dst, sem.at[n])
        for n, (src, dst) in enumerate(
            [(ey_hbm, ey_ref), (v_hbm, v_ref), (ex_hbm, ex_ref), (ix_hbm, ix_ref), (iy_hbm, iy_ref)]
        )
    ]
    column = r_in[:, PER : PER + 8, :].astype(F32)[:, 0, :]
    c_ref[...] = (column * BOX + pltpu.roll(column, LANES - SLOT, 1)).astype(jnp.int32)
    index = pltpu.make_async_copy(c_ref, cell_ref, sem.at[5])
    for copy in fixed:
        copy.start()
    blank = jnp.zeros((4 * BOX, LANES), F32)

    @pl.loop(0, SIDE)
    def _(x):
        g_ref[pl.ds(pl.multiple_of(x * 4 * BOX, 8), 4 * BOX), :] = blank

    index.start()

    @pl.loop(0, NR // 8)
    def _(i):
        for u in range(16):
            for h in range(2):
                s_ref[h, pl.ds((i * 16 + u) * STEP + 64, 8), :] = blank[:8]

    step = 128

    @pl.loop(0, owners // 16)
    def _(i):
        for u in range(16):
            o = i * 16 + u
            f_ref[pl.ds(pl.multiple_of(o * PER, PER), PER), :] = r_in[
                o, 0:PER, :
            ].astype(F32)

    index.wait()

    @pl.loop(0, sticks // step)
    def _(i):
        for u in range(step):
            c = cell_ref[i * (step // SLOT) + u // SLOT, u % SLOT]
            g_ref[pl.ds(pl.multiple_of(4 * c, 4), 4), :] = f_ref[
                pl.ds(pl.multiple_of(i * 4 * step, 4 * step) + 4 * u, 4), :
            ]

    for copy in fixed:
        copy.wait()
    turn = SIDE

    @pl.loop(0, SIDE // turn)
    def _(i):
        xs = []
        for u in range(turn):
            r0 = (i * turn + u) * 4 * BOX
            halves = [
                jnp.concatenate(
                    [g_ref[pl.ds(r0 + 2 * h + p, BOX, stride=4), :] for p in range(2)], axis=0
                )
                for h in range(2)
            ]
            xs.append(jnp.concatenate(halves, axis=1).astype(BF))
        for u in range(turn):
            m = jnp.dot(ey_ref[...], xs[u], preferred_element_type=F32)
            for h in range(2):
                s_ref[h, pl.ds(i * turn + u, 2 * NR, stride=STEP), :] = m[
                    :, h * LANES : (h + 1) * LANES
                ]

    lane = lax.broadcasted_iota(jnp.int32, (NR, NR), 1)
    v = v_ref[...]
    batch = 32

    @pl.loop(0, NR // batch)
    def _(i):
        xs = []
        for u in range(batch):
            r0 = (i * batch + u) * 2 * STEP
            halves = [
                jnp.concatenate(
                    [s_ref[h, pl.ds(r0 + p * STEP, BOX), :] for p in range(2)], axis=0
                )
                for h in range(2)
            ]
            xs.append(jnp.concatenate(halves, axis=1).astype(BF))
        for u in range(batch):
            psi = jnp.dot(ex_ref[...], xs[u], preferred_element_type=F32)
            column = jnp.sum(
                jnp.where(lane == i * batch + u, v, 0.0), axis=1, keepdims=True
            )
            vv = jnp.broadcast_to(column, (NR, 2 * LANES))
            w_ref[u] = (psi * jnp.concatenate([vv, vv], axis=0)).astype(BF)
        for u in range(batch):
            m = jnp.dot(ix_ref[...], w_ref[u], preferred_element_type=F32)
            r0 = (i * batch + u) * 2 * STEP
            for h in range(2):
                for p in range(2):
                    s_ref[h, pl.ds(r0 + p * STEP, BOX), :] = m[
                        p * BOX : (p + 1) * BOX, h * LANES : (h + 1) * LANES
                    ]

    @pl.loop(0, SIDE // turn)
    def _(i):
        xs = []
        for u in range(turn):
            rows = pl.ds(i * turn + u, 2 * NR, stride=STEP)
            xs.append(jnp.concatenate([s_ref[h, rows, :].astype(BF) for h in range(2)], axis=1))
        for u in range(turn):
            m = jnp.dot(iy_ref[...], xs[u], preferred_element_type=F32)
            r0 = (i * turn + u) * 4 * BOX
            for h in range(2):
                for p in range(2):
                    g_ref[pl.ds(r0 + 2 * h + p, BOX, stride=4), :] = m[
                        p * BOX : (p + 1) * BOX, h * LANES : (h + 1) * LANES
                    ]


    @pl.loop(0, sticks // step)
    def _(i):
        for u in range(step):
            c = cell_ref[i * (step // SLOT) + u // SLOT, u % SLOT]
            f_ref[pl.ds(pl.multiple_of(i * 4 * step, 4 * step) + 4 * u, 4), :] = g_ref[
                pl.ds(pl.multiple_of(4 * c, 4), 4), :
            ]

    @pl.loop(0, owners // 16)
    def _(i):
        for u in range(16):
            o = i * 16 + u
            o_ref[o] = f_ref[pl.ds(pl.multiple_of(o * PER, PER), PER), :].astype(BF)


def plane_pass(received, volume, tabs):
    owners = received.shape[0]
    return pl.pallas_call(
        plane_kernel,
        out_shape=jax.ShapeDtypeStruct((owners, PER, LANES), BF),
        in_specs=[VMEM] + [HBM] * 5,
        out_specs=VMEM,
        scratch_shapes=[
            pltpu.VMEM(volume.shape, F32),
            *[pltpu.VMEM(t.shape, BF) for t in tabs],
            pltpu.VMEM((owners * PER, LANES), F32),
            pltpu.VMEM((SIDE * BOX * 4, LANES), F32),
            pltpu.VMEM((2, 2 * NR * STEP, LANES), F32),
            pltpu.VMEM((32, 2 * NR, 2 * LANES), BF),
            pltpu.VMEM((owners, LANES), jnp.int32),
            pltpu.SMEM((owners, LANES), jnp.int32),
            pltpu.SemaphoreType.DMA((6,)),
        ],
        compiler_params=pltpu.CompilerParams(vmem_limit_bytes=48 << 20),
        cost_estimate=pl.CostEstimate(
            flops=2 * 77000 * 256 * 256, bytes_accessed=6 << 20, transcendentals=0
        ),
        name="plane",
    )(received, volume, *tabs)


def finish_kernel(r_ref, place_ref, i_ref, o_hbm, t_ref, sp_ref, out_ref, sem):
    place = place_ref[...]
    count = place.shape[1]
    spot = ((place >> 7) * BOX + ((place + HALF) & (NR - 1))).astype(F32)
    across = lax.broadcasted_iota(jnp.int32, (count, count), 1)
    down = lax.broadcasted_iota(jnp.int32, (count, count), 0)
    row = jnp.sum(jnp.where(across == down, spot, 0.0), axis=1, keepdims=True).astype(jnp.int32)
    at = lax.broadcasted_iota(jnp.int32, (count, SLOT * BOX), 1)
    select = jnp.where(at == row, 1.0 / NR**3, 0.0).astype(BF)

    @pl.loop(0, NR // 8)
    def _(i):
        for u in range(8):
            k = i * 8 + u
            t_ref[pl.ds(k * WIDE, PER), :] = r_ref[k].astype(F32)

    for s in range(SLOT):
        halves = [
            jnp.concatenate(
                [t_ref[pl.ds(4 * s + 2 * h + p, NR, stride=WIDE), :] for p in range(2)], axis=0
            )
            for h in range(2)
        ]
        x = jnp.concatenate(halves, axis=1).astype(BF)
        m = jnp.dot(i_ref[...], x, preferred_element_type=F32)
        for p in range(2):
            sp_ref[p, s * BOX : (s + 1) * BOX, :] = m[p * BOX : (p + 1) * BOX]
    sends = []
    for p in range(2):
        out_ref[p] = jnp.dot(select, sp_ref[p].astype(BF), preferred_element_type=F32)
        sends.append(pltpu.make_async_copy(out_ref.at[p], o_hbm.at[p], sem.at[p]))
        sends[p].start()
    for copy in sends:
        copy.wait()


def finish(returned, place, behind_z):
    out = jax.ShapeDtypeStruct((2, place.shape[1], 2 * LANES), F32)
    return pl.pallas_call(
        finish_kernel,
        out_shape=out,
        in_specs=[VMEM] * 3,
        out_specs=HBM,
        scratch_shapes=[
            pltpu.VMEM((NR * WIDE, LANES), F32),
            pltpu.VMEM((2, SLOT * BOX, 2 * LANES), F32),
            pltpu.VMEM(out.shape, F32),
            pltpu.SemaphoreType.DMA((2,)),
        ],
        compiler_params=pltpu.CompilerParams(vmem_limit_bytes=24 << 20),
        cost_estimate=pl.CostEstimate(
            flops=2 * (2304 + 2560) * 256 * 256, bytes_accessed=3 << 20, transcendentals=0
        ),
        name="finish",
    )(returned, place, behind_z)


def exchange(value):
    return lax.all_to_all(value, TG_PW, split_axis=0, concat_axis=0, tiled=True)


def body(coeffs, g_place, stick_column, potential):
    ahead_x, behind_x, behind_y, ahead_y = tables()
    place = g_place.reshape(1, -1)
    sent = spread(coeffs, place, stick_column, ahead_x)
    got = exchange(sent)
    volume = potential.reshape(NR, NR)
    done = plane_pass(got, volume, (ahead_y, ahead_x, behind_x, behind_y))
    return finish(exchange(done), place, behind_x)


def solution(mesh):
    torus = Mesh(mesh.devices.reshape(mesh.shape["tg"], 4, 4, 4), ("tg", "pw_0", "pw_1", "pw_2"))
    return jax.shard_map(
        body,
        mesh=torus,
        in_specs=(P(None, TG_PW, None), P(TG_PW), P(TG_PW), P(None, None, TG_PW)),
        out_specs=P(None, TG_PW, None),
        check_vma=False,
    )
```

```python
import functools

import numpy as np
import jax
import jax.numpy as jnp
from jax import lax
from jax.experimental import pallas as pl
from jax.experimental.pallas import tpu as pltpu
from jax.sharding import Mesh
from jax.sharding import PartitionSpec as P

NR = 128
HALF = 32
BOX = 72
SIDE = 65
STEP = 73
SLOT = 16
LANES = 128
PER = 4 * SLOT
WIDE = PER + 1
PIECES = 4
TG_PW = ("tg", "pw_0", "pw_1", "pw_2")
BF = jnp.bfloat16
F32 = jnp.float32
VMEM = pl.BlockSpec(memory_space=pltpu.VMEM)
HBM = pl.BlockSpec(memory_space=pltpu.HBM)
SMEM = pl.BlockSpec(memory_space=pltpu.SMEM)


def complex_table(rows, cols, sign, keep_rows, keep_cols):
    angle = 2.0 * np.pi / NR * (np.outer(rows, cols) % NR)
    keep = keep_rows[:, None] * keep_cols[None, :]
    c = np.cos(angle) * keep
    s = sign * np.sin(angle) * keep
    return np.stack([np.stack([c, -s], 1), np.stack([s, c], 1)]).astype(np.float32)


def tables():
    full = np.arange(NR)
    box = np.arange(BOX) - HALF
    keep_box = (np.arange(BOX) <= 2 * HALF).astype(np.float32)
    keep_all = np.ones(NR, np.float32)
    ahead = complex_table(full, box, 1.0, keep_all, keep_box)
    behind = complex_table(box, full, -1.0, keep_box, keep_all)
    wide, tall = 2 * NR, 2 * BOX
    ahead_x = ahead.reshape(wide, tall)
    behind_x = behind.reshape(tall, wide)
    behind_y = behind.transpose(0, 1, 3, 2).reshape(tall, wide)
    ahead_y = ahead.transpose(1, 0, 2, 3).reshape(wide, tall)
    return [jnp.asarray(t, BF) for t in (ahead_x, behind_x, behind_y, ahead_y)]


def spread_kernel(
    c_hbm, place_hbm, column_ref, e_hbm, o_hbm, c_ref, place_ref, e_ref, t_ref, o_ref, sem
):
    first = pltpu.make_async_copy(place_hbm, place_ref, sem.at[PIECES])
    first.start()
    copies = [pltpu.make_async_copy(c_hbm.at[p], c_ref.at[p], sem.at[p]) for p in range(2)]
    copies.append(pltpu.make_async_copy(e_hbm, e_ref, sem.at[2]))
    for copy in copies:
        copy.start()
    first.wait()
    place = place_ref[...]
    row = (place >> 7) * BOX + ((place + HALF) & (NR - 1))
    at = lax.broadcasted_iota(jnp.int32, (SLOT * BOX, place.shape[1]), 0)
    select = jnp.where(at == row, 1.0, 0.0).astype(BF)
    lane = lax.broadcasted_iota(jnp.int32, (8, LANES), 1)
    info = jnp.zeros((8, LANES), jnp.int32)
    for s in range(SLOT):
        column = column_ref[s]
        info = jnp.where(lane == s, ((column >> 7) + HALF) & (NR - 1), info)
        info = jnp.where(lane == SLOT + s, (column + HALF) & (NR - 1), info)
    info = info.astype(F32).astype(BF)
    for copy in copies:
        copy.wait()
    both = jnp.concatenate([c_ref[p].astype(BF) for p in range(2)], axis=1)
    placed = jnp.dot(select, both, preferred_element_type=F32)
    xs = []
    for s in range(SLOT):
        rows = placed[s * BOX : (s + 1) * BOX]
        xs.append(
            jnp.concatenate([rows[:, : 2 * LANES], rows[:, 2 * LANES :]], axis=0).astype(BF)
        )
    for s in range(SLOT):
        m = jnp.dot(e_ref[...], xs[s], preferred_element_type=F32)
        for h in range(2):
            for p in range(2):
                t_ref[pl.ds(4 * s + 2 * h + p, NR, stride=WIDE), :] = m[
                    p * NR : (p + 1) * NR, h * LANES : (h + 1) * LANES
                ]
    share = NR // PIECES
    sends = []
    for q in range(PIECES):

        @pl.loop(q * share // 8, (q + 1) * share // 8)
        def _(i):
            for u in range(8):
                k = i * 8 + u
                o_ref[k, 0:PER, :] = t_ref[pl.ds(k * WIDE, PER), :].astype(BF)
                o_ref[k, PER : PER + 8, :] = info

        part = pl.ds(q * share, share)
        sends.append(pltpu.make_async_copy(o_ref.at[part], o_hbm.at[part], sem.at[q]))
        sends[q].start()
    for copy in sends:
        copy.wait()


def spread(coeffs, place, columns, ahead_z):
    out = jax.ShapeDtypeStruct((NR, PER + 8, LANES), BF)
    return pl.pallas_call(
        spread_kernel,
        out_shape=out,
        in_specs=[HBM, HBM, SMEM, HBM],
        out_specs=HBM,
        scratch_shapes=[
            pltpu.VMEM(coeffs.shape, F32),
            pltpu.VMEM(place.shape, jnp.int32),
            pltpu.VMEM(ahead_z.shape, BF),
            pltpu.VMEM((NR * WIDE, LANES), F32),
            pltpu.VMEM(out.shape, BF),
            pltpu.SemaphoreType.DMA((PIECES + 1,)),
        ],
        compiler_params=pltpu.CompilerParams(vmem_limit_bytes=62 << 20),
        cost_estimate=pl.CostEstimate(
            flops=2 * (2304 + 4096) * 256 * 256, bytes_accessed=3 << 20, transcendentals=0
        ),
        name="spread",
    )(coeffs, place, columns, ahead_z)


def plane_kernel(
    cell_ref, r_in, v_hbm, ey_hbm, ex_hbm, ix_hbm, iy_hbm, o_ref,
    v_ref, ey_ref, ex_ref, ix_ref, iy_ref, f_ref, g_ref, s_ref, w_ref, sem,
):
    owners = o_ref.shape[0]
    sticks = owners * SLOT
    share = owners // PIECES
    fixed = [
        pltpu.make_async_copy(src, dst, sem.at[n])
        for n, (src, dst) in enumerate(
            [(ey_hbm, ey_ref), (v_hbm, v_ref), (ex_hbm, ex_ref), (ix_hbm, ix_ref), (iy_hbm, iy_ref)]
        )
    ]
    for copy in fixed:
        copy.start()
    blank = jnp.zeros((4 * BOX, LANES), F32)

    @pl.loop(0, SIDE)
    def _(x):
        g_ref[pl.ds(pl.multiple_of(x * 4 * BOX, 8), 4 * BOX), :] = blank

    @pl.loop(0, NR // 8)
    def _(i):
        for u in range(16):
            for h in range(2):
                s_ref[h, pl.ds((i * 16 + u) * STEP + 64, 8), :] = blank[:8]

    step = 128
    for q in range(PIECES):

        @pl.loop(q * share // 16, (q + 1) * share // 16)
        def _(i):
            for u in range(16):
                o = i * 16 + u
                f_ref[pl.ds(pl.multiple_of(o * PER, PER), PER), :] = r_in[
                    o, 0:PER, :
                ].astype(F32)

        @pl.loop(q * sticks // PIECES // step, (q + 1) * sticks // PIECES // step)
        def _(i):
            for u in range(step):
                c = cell_ref[i * step + u]
                g_ref[pl.ds(pl.multiple_of(c, 4), 4), :] = f_ref[
                    pl.ds(pl.multiple_of(i * 4 * step, 4 * step) + 4 * u, 4), :
                ]

    for copy in fixed:
        copy.wait()
    turn = SIDE

    @pl.loop(0, SIDE // turn)
    def _(i):
        xs = []
        for u in range(turn):
            r0 = (i * turn + u) * 4 * BOX
            halves = [
                jnp.concatenate(
                    [g_ref[pl.ds(r0 + 2 * h + p, BOX, stride=4), :] for p in range(2)], axis=0
                )
                for h in range(2)
            ]
            xs.append(jnp.concatenate(halves, axis=1).astype(BF))
        for u in range(turn):
            m = jnp.dot(ey_ref[...], xs[u], preferred_element_type=F32)
            for h in range(2):
                s_ref[h, pl.ds(i * turn + u, 2 * NR, stride=STEP), :] = m[
                    :, h * LANES : (h + 1) * LANES
                ]

    lane = lax.broadcasted_iota(jnp.int32, (NR, NR), 1)
    v = v_ref[...]
    batch = 32

    @pl.loop(0, NR // batch)
    def _(i):
        xs = []
        for u in range(batch):
            r0 = (i * batch + u) * 2 * STEP
            halves = [
                jnp.concatenate(
                    [s_ref[h, pl.ds(r0 + p * STEP, BOX), :] for p in range(2)], axis=0
                )
                for h in range(2)
            ]
            xs.append(jnp.concatenate(halves, axis=1).astype(BF))
        for u in range(batch):
            psi = jnp.dot(ex_ref[...], xs[u], preferred_element_type=F32)
            column = jnp.sum(
                jnp.where(lane == i * batch + u, v, 0.0), axis=1, keepdims=True
            )
            vv = jnp.broadcast_to(column, (NR, 2 * LANES))
            w_ref[u] = (psi * jnp.concatenate([vv, vv], axis=0)).astype(BF)
        for u in range(batch):
            m = jnp.dot(ix_ref[...], w_ref[u], preferred_element_type=F32)
            r0 = (i * batch + u) * 2 * STEP
            for h in range(2):
                for p in range(2):
                    s_ref[h, pl.ds(r0 + p * STEP, BOX), :] = m[
                        p * BOX : (p + 1) * BOX, h * LANES : (h + 1) * LANES
                    ]

    @pl.loop(0, SIDE // turn)
    def _(i):
        xs = []
        for u in range(turn):
            rows = pl.ds(i * turn + u, 2 * NR, stride=STEP)
            xs.append(jnp.concatenate([s_ref[h, rows, :].astype(BF) for h in range(2)], axis=1))
        for u in range(turn):
            m = jnp.dot(iy_ref[...], xs[u], preferred_element_type=F32)
            r0 = (i * turn + u) * 4 * BOX
            for h in range(2):
                for p in range(2):
                    g_ref[pl.ds(r0 + 2 * h + p, BOX, stride=4), :] = m[
                        p * BOX : (p + 1) * BOX, h * LANES : (h + 1) * LANES
                    ]

    for q in range(PIECES):

        @pl.loop(q * sticks // PIECES // step, (q + 1) * sticks // PIECES // step)
        def _(i):
            for u in range(step):
                c = cell_ref[i * step + u]
                f_ref[pl.ds(pl.multiple_of(i * 4 * step, 4 * step) + 4 * u, 4), :] = g_ref[
                    pl.ds(pl.multiple_of(c, 4), 4), :
                ]

        @pl.loop(q * share // 16, (q + 1) * share // 16)
        def _(i):
            for u in range(16):
                o = i * 16 + u
                o_ref[o] = f_ref[pl.ds(pl.multiple_of(o * PER, PER), PER), :].astype(BF)


def plane_pass(cells, received, volume, tabs):
    owners = received.shape[0]
    return pl.pallas_call(
        plane_kernel,
        out_shape=jax.ShapeDtypeStruct((owners, PER, LANES), BF),
        in_specs=[SMEM, VMEM] + [HBM] * 5,
        out_specs=VMEM,
        scratch_shapes=[
            pltpu.VMEM(volume.shape, F32),
            *[pltpu.VMEM(t.shape, BF) for t in tabs],
            pltpu.VMEM((owners * PER, LANES), F32),
            pltpu.VMEM((SIDE * BOX * 4, LANES), F32),
            pltpu.VMEM((2, 2 * NR * STEP, LANES), F32),
            pltpu.VMEM((32, 2 * NR, 2 * LANES), BF),
            pltpu.SemaphoreType.DMA((5,)),
        ],
        compiler_params=pltpu.CompilerParams(vmem_limit_bytes=48 << 20),
        cost_estimate=pl.CostEstimate(
            flops=2 * 77000 * 256 * 256, bytes_accessed=6 << 20, transcendentals=0
        ),
        name="plane",
    )(cells, received, volume, *tabs)


def finish_kernel(r_ref, place_ref, i_ref, o_hbm, t_ref, sp_ref, out_ref, sem):
    place = place_ref[...]
    count = place.shape[1]
    spot = ((place >> 7) * BOX + ((place + HALF) & (NR - 1))).astype(F32)
    across = lax.broadcasted_iota(jnp.int32, (count, count), 1)
    down = lax.broadcasted_iota(jnp.int32, (count, count), 0)
    row = jnp.sum(jnp.where(across == down, spot, 0.0), axis=1, keepdims=True).astype(jnp.int32)
    at = lax.broadcasted_iota(jnp.int32, (count, SLOT * BOX), 1)
    select = jnp.where(at == row, 1.0 / NR**3, 0.0).astype(BF)

    @pl.loop(0, NR // 8)
    def _(i):
        for u in range(8):
            k = i * 8 + u
            t_ref[pl.ds(k * WIDE, PER), :] = r_ref[k].astype(F32)

    for s in range(SLOT):
        halves = [
            jnp.concatenate(
                [t_ref[pl.ds(4 * s + 2 * h + p, NR, stride=WIDE), :] for p in range(2)], axis=0
            )
            for h in range(2)
        ]
        x = jnp.concatenate(halves, axis=1).astype(BF)
        m = jnp.dot(i_ref[...], x, preferred_element_type=F32)
        for p in range(2):
            sp_ref[p, s * BOX : (s + 1) * BOX, :] = m[p * BOX : (p + 1) * BOX]
    sends = []
    for p in range(2):
        out_ref[p] = jnp.dot(select, sp_ref[p].astype(BF), preferred_element_type=F32)
        sends.append(pltpu.make_async_copy(out_ref.at[p], o_hbm.at[p], sem.at[p]))
        sends[p].start()
    for copy in sends:
        copy.wait()


def finish(returned, place, behind_z):
    out = jax.ShapeDtypeStruct((2, place.shape[1], 2 * LANES), F32)
    return pl.pallas_call(
        finish_kernel,
        out_shape=out,
        in_specs=[VMEM] * 3,
        out_specs=HBM,
        scratch_shapes=[
            pltpu.VMEM((NR * WIDE, LANES), F32),
            pltpu.VMEM((2, SLOT * BOX, 2 * LANES), F32),
            pltpu.VMEM(out.shape, F32),
            pltpu.SemaphoreType.DMA((2,)),
        ],
        compiler_params=pltpu.CompilerParams(vmem_limit_bytes=24 << 20),
        cost_estimate=pl.CostEstimate(
            flops=2 * (2304 + 2560) * 256 * 256, bytes_accessed=3 << 20, transcendentals=0
        ),
        name="finish",
    )(returned, place, behind_z)


def exchange(value):
    return lax.all_to_all(value, TG_PW, split_axis=0, concat_axis=0, tiled=True)


def body(coeffs, g_place, stick_column, potential):
    ahead_x, behind_x, behind_y, ahead_y = tables()
    place = g_place.reshape(1, -1)
    sent = spread(coeffs, place, stick_column, ahead_x)
    got = exchange(sent)
    column = got[:, PER, : 2 * SLOT].astype(F32).astype(jnp.int32)
    cells = (column[:, :SLOT] * (4 * BOX) + column[:, SLOT:] * 4).reshape(-1)
    volume = potential.reshape(NR, NR)
    done = plane_pass(cells, got, volume, (ahead_y, ahead_x, behind_x, behind_y))
    return finish(exchange(done), place, behind_x)


def solution(mesh):
    torus = Mesh(mesh.devices.reshape(mesh.shape["tg"], 4, 4, 4), ("tg", "pw_0", "pw_1", "pw_2"))
    return jax.shard_map(
        body,
        mesh=torus,
        in_specs=(P(None, TG_PW, None), P(TG_PW), P(TG_PW), P(None, None, TG_PW)),
        out_specs=P(None, TG_PW, None),
        check_vma=False,
    )
```
